256 devices in a mesh: group: 8 (over y, x_lo), member: 32 (over x_hi, z, core).
Axes of the slice: x: 4 (x_hi: 2, x_lo: 2; x = x_hi * 2 + x_lo), y: 4, z: 8, core: 2. Of those that a mesh axis runs over, the one named last changes fastest.
Arguments:
- clips: bfloat16 [256, 14, 64, 640], P(('group', 'member')), may hold values from -4 to 4
- targets: bfloat16 [256, 14, 64, 640], P(('group', 'member')), may hold values from -6 to 6
- timestep: int32 [256], P(('group', 'member')), may hold values from 0 to 999
- identity: int32 [256], P(('group', 'member')), may hold values from 0 to 63
- conv1_weight: bfloat16 [1920, 640], P('member', 'group'), may hold values from -6 to 6
- conv2_weight: bfloat16 [1920, 640], P('member', 'group'), may hold values from -6 to 6
- rate1: bfloat16 [1920, 640], P('member', 'group'), may hold values from 0.029907227 to 0.29882812
- rate2: bfloat16 [1920, 640], P('member', 'group'), may hold values from 0.029907227 to 0.29882812
- time_proj: bfloat16 [1280, 640], replicated, may hold values from -0.15625 to 0.15625
- subject_table: float32 [64, 1280], replicated, may hold values from -6 to 6
Outputs:
- adapted_first: float32 [8, 1920, 640], P('group', 'member')
- adapted_second: float32 [8, 1920, 640], P('group', 'member')
The draws below stay inside these ranges and needn't reach their ends.
All inputs are finite; a program needn't handle non-finite values.
Results may differ from the reference program's by a relative error of at most 0.0016.
Values may be sent and summed in bfloat16 or wider, within the bound.
A program may use at most 128 MiB of HBM per device.

```python
import math
import jax
import jax.numpy as jnp
from jax import lax

C = 640
TEMB = 1280
FRAMES = 14
HW = 64
GN_GROUPS = 32
IDENTS = 64
CLIPS = 256
N_GROUP = 8
N_MEMBER = 32


def draw_clips(key, part):
    key_values, key_channel, key_position = jax.random.split(key, 3)
    reach = math.log(10.0)
    channel_scale = jnp.exp(jax.random.uniform(key_channel, (CLIPS, 1, 1, C), jnp.float32, -reach, 0.0))
    position_scale = jnp.exp(jax.random.uniform(key_position, (CLIPS, FRAMES, HW, 1), jnp.float32, -reach, 0.0))
    rough = jax.random.truncated_normal(key_values, -4.0, 4.0, (CLIPS, FRAMES, HW, C), jnp.float32)
    values = rough * channel_scale * position_scale
    return values.astype(jnp.bfloat16)


def plant(drawn, rng, smallest, high):
    dims = drawn.shape
    place = [jax.random.randint(jax.random.fold_in(rng, axis), (), 0, dims[axis]) for axis in range(len(dims))]
    drawn = drawn.at[tuple(place)].set(smallest)
    longest = dims.index(max(dims))
    place[longest] = (place[longest] + 1) % dims[longest]
    return drawn.at[tuple(place)].set(high)


def steps_of(key, dims, pieces, smallest, top_value):
    def one(position, blocks):
        draws = jax.random.uniform(jax.random.fold_in(jax.random.fold_in(key, 6), position), (blocks,), jnp.float32, smallest / len(pieces), top_value / len(pieces))
        return jnp.repeat(jnp.exp(draws), dims[position] // blocks).reshape((-1,) + (1,) * (len(dims) - position - 1))

    loudness = one(*pieces[0])
    for cut in pieces[1:]:
        loudness = loudness * one(*cut)
    return loudness


def normal_values(key, extent, scale, bound, cuts=(), held_as=jnp.bfloat16):
    drawn = scale * jax.random.normal(key, extent, jnp.float32)
    if cuts:
        drawn = drawn * steps_of(key, extent, cuts, -0.22, 0.18)
    return jnp.clip(drawn, -bound, bound).astype(held_as)


def setup_inputs(seed: int = 0) -> dict:
    seeds = jax.random.split(jax.random.key(seed), 11)
    clips = draw_clips(jax.random.fold_in(seeds[10], 71), 0)
    targets = normal_values(seeds[1], (CLIPS, FRAMES, HW, C), 1.0, 6.0, ((0, 256),))
    timestep = plant(jax.random.randint(seeds[2], (CLIPS,), 0, 1000), jax.random.fold_in(seeds[2], 1), 0, 999).astype(jnp.int32)
    identity = plant(jax.random.randint(seeds[3], (CLIPS,), 0, IDENTS), jax.random.fold_in(seeds[3], 1), 0, IDENTS - 1).astype(jnp.int32)
    conv1_weight = normal_values(seeds[4], (3 * C, C), 1.0, 6.0, ((0, 32), (1, 8)))
    conv2_weight = normal_values(seeds[5], (3 * C, C), 1.0, 6.0, ((0, 32), (1, 8)))
    rate1 = jnp.clip(jnp.exp(math.log(0.29882812) - 2.30176843 * jax.random.uniform(seeds[6], (3 * C, C), jnp.float32) ** steps_of(seeds[6], (3 * C, C), ((0, 32), (1, 8)), -0.2, 0.2)), 0.029907227, 0.29882812).astype(jnp.bfloat16)
    rate2 = jnp.clip(jnp.exp(math.log(0.29882812) - 2.30176843 * jax.random.uniform(seeds[7], (3 * C, C), jnp.float32) ** steps_of(seeds[7], (3 * C, C), ((0, 32), (1, 8)), -0.2, 0.2)), 0.029907227, 0.29882812).astype(jnp.bfloat16)
    time_proj = normal_values(seeds[8], (TEMB, C), TEMB ** -0.5, 0.15625)
    subject_table = normal_values(seeds[9], (IDENTS, TEMB), 1.0, 6.0, (), jnp.float32)
    return {"clips": clips, "targets": targets, "timestep": timestep, "identity": identity, "conv1_weight": conv1_weight, "conv2_weight": conv2_weight, "rate1": rate1, "rate2": rate2, "time_proj": time_proj, "subject_table": subject_table}


def time_bias(step_index, ident, subject_table, time_proj):
    half_width = subject_table.shape[1] // 2
    freqs = jnp.exp(-math.log(10000.0) * jnp.arange(half_width, dtype=jnp.float32) / half_width)
    angles = step_index.astype(jnp.float32) * freqs
    embedding = jnp.concatenate([jnp.cos(angles), jnp.sin(angles)])
    onehot = (jnp.arange(subject_table.shape[0], dtype=jnp.int32) == ident.astype(jnp.int32)).astype(jnp.float32)
    embedding = embedding + jnp.dot(onehot, subject_table, precision=lax.Precision.HIGHEST)
    activated = jax.nn.silu(embedding).astype(jnp.bfloat16)
    return jnp.dot(activated[None, :], time_proj, preferred_element_type=jnp.float32)[0]

def group_norm(values):
    channels = values.shape[2]
    per_group = channels // GN_GROUPS
    counted = values.shape[0] * values.shape[1] * per_group

    def spread(sums):
        return jnp.repeat(sums.reshape(GN_GROUPS, per_group).sum(axis=1) / counted, per_group)
    centre = spread(values.sum(axis=(0, 1)))
    centred = values - centre
    variance = spread((centred * centred).sum(axis=(0, 1)))
    return centred * lax.rsqrt(variance + 1e-05)

def activate(values):
    return jax.nn.silu(group_norm(values))

def stack_taps(act_values):
    frames, points, channels = act_values.shape
    blank = jnp.zeros((1, points, channels), act_values.dtype)
    before = jnp.concatenate([blank, act_values[:-1]], axis=0)
    after = jnp.concatenate([act_values[1:], blank], axis=0)
    return jnp.concatenate([before, act_values, after], axis=2).reshape(frames * points, 3 * channels)

def fold_taps(grad_rows, frames, points, channels):
    shaped = grad_rows.reshape(frames, points, 3 * channels)
    blank = jnp.zeros((1, points, channels), jnp.float32)
    from_before = jnp.concatenate([shaped[1:, :, :channels], blank], axis=0)
    from_after = jnp.concatenate([blank, shaped[:-1, :, 2 * channels:]], axis=0)
    return shaped[:, :, channels:2 * channels] + from_before + from_after

def clip_grads(clip, target, step_index, ident, conv1_weight, conv2_weight, time_proj, subject_table):
    weight_scale = 1.0 / math.sqrt(3 * C)
    latent = clip.astype(jnp.float32)
    bias_row = time_bias(step_index, ident, subject_table, time_proj)
    stacked_one = stack_taps(activate(latent).astype(jnp.bfloat16))
    hidden = weight_scale * jnp.dot(stacked_one, conv1_weight, preferred_element_type=jnp.float32) + bias_row
    hidden = hidden.reshape(FRAMES, HW, C)
    act_two, backward = jax.vjp(activate, hidden)
    stacked_two = stack_taps(act_two.astype(jnp.bfloat16))
    mixed_two = jnp.dot(stacked_two, conv2_weight, preferred_element_type=jnp.float32)
    output = latent + (weight_scale * mixed_two).reshape(FRAMES, HW, C)
    error = (output - target.astype(jnp.float32)).reshape(FRAMES * HW, C).astype(jnp.bfloat16)
    back_rows = lax.dot_general(error, conv2_weight, (((1,), (1,)), ((), ())), preferred_element_type=jnp.float32)
    grad_act = fold_taps(weight_scale * back_rows, FRAMES, HW, C)
    grad_hidden = backward(grad_act)[0].reshape(FRAMES * HW, C).astype(jnp.bfloat16)
    first_dims = (((0,), (0,)), ((), ()))
    grad_one = weight_scale * lax.dot_general(stacked_one, grad_hidden, first_dims, preferred_element_type=jnp.float32)
    grad_two = weight_scale * lax.dot_general(stacked_two, error, first_dims, preferred_element_type=jnp.float32)
    return (grad_one, grad_two)

def reference(clips, targets, timestep, identity, conv1_weight, conv2_weight, rate1, rate2, time_proj, subject_table):

    def by_group(array):
        return array.reshape((N_GROUP, N_MEMBER) + array.shape[1:])

    def group_grads(items):

        def accumulate(running, single):
            grad_one, grad_two = clip_grads(single[0], single[1], single[2], single[3], conv1_weight, conv2_weight, time_proj, subject_table)
            return ((running[0] + grad_one, running[1] + grad_two), None)
        empty_sum = jnp.zeros((3 * C, C), jnp.float32)
        summed, unused = lax.scan(accumulate, (empty_sum, empty_sum), items)
        return summed
    grad_first, grad_second = lax.map(group_grads, (by_group(clips), by_group(targets), by_group(timestep), by_group(identity)))
    adapted_first = conv1_weight.astype(jnp.float32)[None] - rate1.astype(jnp.float32)[None] * grad_first
    adapted_second = conv2_weight.astype(jnp.float32)[None] - rate2.astype(jnp.float32)[None] * grad_second
    return (adapted_first, adapted_second)
```

```python
import functools
import math

import jax
import jax.numpy as jnp
from jax import lax
from jax.experimental import pallas as pl
from jax.experimental.pallas import tpu as pltpu
from jax.sharding import PartitionSpec as P

GN_GROUPS = 32
MESH = pl.DeviceIdType.MESH
N_GROUP, N_MEMBER, NZ, NC, NX = 8, 32, 8, 2, 2
ROWS, COLS, C = 60, 80, 640
TAPS = 3 * C


class Place:
    def __init__(self):
        self.g = lax.axis_index("group")
        self.m = lax.axis_index("member")
        self.core = lax.rem(self.m, 2)
        self.q = lax.div(self.m, 2)
        self.z = lax.rem(self.q, NZ)
        self.xh = lax.div(self.q, NZ)
        self.up = self.at(self.xh, self.zof(1), self.core)
        self.down = self.at(self.xh, self.zof(-1), self.core)
        self.across = self.at(1 - self.xh, self.z, self.core)
        self.sibling = self.at(self.xh, self.z, 1 - self.core)

    def at(self, xh, z, core):
        return (self.g, (xh * NZ + z) * 2 + core)

    def zof(self, step):
        return lax.rem(self.z + (step + NZ), NZ)

    def peer(self, step):
        return lax.rem(self.g + step, N_GROUP)

    def xof(self, piece):
        return self.xh if piece == 0 else 1 - self.xh


def remote(src, dst, send, recv, device):
    return pltpu.make_async_remote_copy(
        src_ref=src, dst_ref=dst, send_sem=send, recv_sem=recv, device_id=device, device_id_type=MESH
    )


def enter(place, with_group):
    barrier = pltpu.get_barrier_semaphore()
    partners = [place.up, place.down, place.across, place.sibling]
    if with_group:
        partners += [(place.peer(step), place.m) for step in range(1, N_GROUP)]
    for partner in partners:
        pl.semaphore_signal(barrier, inc=1, device_id=partner, device_id_type=MESH)
    pl.semaphore_wait(barrier, len(partners))


def gather_kernel(w1, w2, r1, r2, d1, d2, own_out, gbuf, wbuf, gsend, grecv, zsend, zrecv, xsend, xrecv, ssend, srecv):
    place = Place()
    for index, ref in enumerate((w1, w2, r1, r2)):
        gbuf[index, place.g] = ref[...]
    enter(place, True)
    sends = []

    def group_copy(part, step, here):
        block = pl.ds(part, 1) if part < 2 else pl.ds(2, 2)
        source = place.g if here else lax.rem(place.g + (N_GROUP - step), N_GROUP)
        ref = gbuf.at[block, source]
        return remote(ref, ref, gsend.at[part, step], grecv.at[part, step], (place.peer(step), place.m))

    for part in range(3):
        for step in range(1, N_GROUP):
            copy = group_copy(part, step, True)
            copy.start()
            sends.append(copy)

    def assemble(index):
        blocks = [gbuf[index, group].astype(jnp.float32) for group in range(N_GROUP)]
        return jnp.concatenate(blocks, axis=1).astype(jnp.bfloat16)

    def slot(w, dist, piece):
        return wbuf.at[w, place.xof(piece), place.zof(-dist), place.core]

    def share(w, dist, piece):
        ref = slot(w, dist, piece)
        copy = remote(ref, ref, ssend.at[w, dist % NZ, piece], srecv.at[w, dist % NZ, piece], place.sibling)
        copy.start()
        sends.append(copy)

    def hop(w, direction, dist, piece):
        sign = 1 if direction == 0 else -1
        ref = slot(w, sign * (dist - 1), piece)
        to = place.up if direction == 0 else place.down
        return remote(ref, ref, zsend.at[w, direction, dist, piece], zrecv.at[w, direction, dist, piece], to)

    def hop_in(w, direction, dist, piece):
        sign = 1 if direction == 0 else -1
        ref = slot(w, sign * dist, piece)
        to = place.up if direction == 0 else place.down
        return remote(ref, ref, zsend.at[w, direction, dist, piece], zrecv.at[w, direction, dist, piece], to)

    def exists(direction, dist, piece):
        return dist < 4 or (dist == 4 and piece == direction)

    def forward(w, direction, dist, piece):
        if exists(direction, dist, piece):
            copy = hop(w, direction, dist, piece)
            copy.start()
            sends.append(copy)

    def ring(w):
        for step in range(1, N_GROUP):
            group_copy(w, step, False).wait_recv()
        whole = assemble(w)
        own_out[w] = whole
        wbuf[w, place.xh, place.z, place.core] = whole
        mine = slot(w, 0, 0)
        copy = remote(mine, mine, xsend.at[w], xrecv.at[w], place.across)
        copy.start()
        sends.append(copy)
        for direction in range(2):
            forward(w, direction, 1, 0)
        share(w, 0, 0)
        yield
        theirs = slot(w, 0, 1)
        remote(theirs, theirs, xsend.at[w], xrecv.at[w], place.across).wait_recv()
        for direction in range(2):
            forward(w, direction, 1, 1)
        share(w, 0, 1)
        yield
        for dist in range(1, 5):
            for piece in range(2):
                for direction in range(2):
                    if exists(direction, dist, piece):
                        hop_in(w, direction, dist, piece).wait_recv()
                        forward(w, direction, dist + 1, piece)
                        share(w, dist if direction == 0 else -dist, piece)
                        yield
        for dist in range(NZ):
            for piece in range(2):
                ref = wbuf.at[w, place.xof(piece), place.zof(-dist), 1 - place.core]
                remote(ref, ref, ssend.at[w, dist, piece], srecv.at[w, dist, piece], place.sibling).wait_recv()
        yield

    def dense(w, out):
        for m in range(N_MEMBER):
            out[ROWS * m : ROWS * (m + 1), :] = wbuf[w, m // 16, (m // 2) % NZ, m % 2]

    for _ in ring(0):
        pass
    dense(0, d1)
    for _ in ring(1):
        pass
    dense(1, d2)
    for step in range(1, N_GROUP):
        group_copy(2, step, False).wait_recv()
    own_out[2] = assemble(2)
    own_out[3] = assemble(3)
    for copy in sends:
        copy.wait_send()


def gather(w1, w2, r1, r2):
    bf16 = jnp.bfloat16
    dma = pltpu.SemaphoreType.DMA
    vmem = pl.BlockSpec(memory_space=pltpu.VMEM)
    return pl.pallas_call(
        gather_kernel,
        out_shape=(
            jax.ShapeDtypeStruct((TAPS, C), bf16),
            jax.ShapeDtypeStruct((TAPS, C), bf16),
            jax.ShapeDtypeStruct((4, ROWS, C), bf16),
        ),
        in_specs=[vmem] * 4,
        out_specs=(vmem,) * 3,
        scratch_shapes=[
            pltpu.VMEM((4, N_GROUP, ROWS, COLS), bf16),
            pltpu.VMEM((2, NX, NZ, NC, ROWS, C), bf16),
            dma((3, N_GROUP)),
            dma((3, N_GROUP)),
            dma((2, 2, 5, 2)),
            dma((2, 2, 5, 2)),
            dma((2,)),
            dma((2,)),
            dma((2, NZ, 2)),
            dma((2, NZ, 2)),
        ],
        compiler_params=pltpu.CompilerParams(
            collective_id=0, has_side_effects=True, vmem_limit_bytes=48 << 20
        ),
        name="gather_weights",
    )(w1, w2, r1, r2)


def reduce_kernel(g1, g2, own, o1, o2, blocks, sib_out, sib_in, hop_out, hop_in, last_out, last_in, x_out, x_in,
                  ssend, srecv, zsend, zrecv, xsend, xrecv):
    place = Place()
    enter(place, False)
    sends = []
    order = [4, 3, 5, 2, 6, 1, 7, 0]

    def lay(w, grad):
        for m in range(N_MEMBER):
            blocks[w, m // 16, (m // 2) % NZ, m % 2] = grad[ROWS * m : ROWS * (m + 1), :]

    def pair(w):
        for dist in order:
            for piece in range(2):
                sib_out[w, dist, piece] = blocks[w, place.xof(piece), place.zof(dist), 1 - place.core].astype(sib_out.dtype)
                copy = remote(sib_out.at[w, dist, piece], sib_in.at[w, dist, piece],
                              ssend.at[w, dist, piece], srecv.at[w, dist, piece], place.sibling)
                copy.start()
                sends.append(copy)

    def summed(w, dist, piece):
        remote(sib_out.at[w, dist, piece], sib_in.at[w, dist, piece],
               ssend.at[w, dist, piece], srecv.at[w, dist, piece], place.sibling).wait_recv()
        return (blocks[w, place.xof(piece), place.zof(dist), place.core]
                + sib_in[w, dist, piece].astype(jnp.float32))

    def exists(direction, dist, piece):
        return dist < 4 or (dist == 4 and piece == direction)

    def hop(w, direction, dist, piece):
        to = place.up if direction == 0 else place.down
        if dist == 1:
            src, dst = last_out.at[w, direction, piece], last_in.at[w, direction, piece]
        else:
            src, dst = hop_out.at[w, direction, dist - 2, piece], hop_in.at[w, direction, dist - 2, piece]
        return src, dst, remote(src, dst, zsend.at[w, direction, dist, piece], zrecv.at[w, direction, dist, piece], to)

    def scatter(w):
        for dist in (4, 3, 2, 1):
            for piece in range(2):
                for direction in range(2):
                    if not exists(direction, dist, piece):
                        continue
                    total = summed(w, dist if direction == 0 else NZ - dist, piece)
                    if exists(direction, dist + 1, piece):
                        _, arrived, copy = hop(w, direction, dist + 1, piece)
                        copy.wait_recv()
                        total = total + arrived[...].astype(jnp.float32)
                    src, _, copy = hop(w, direction, dist, piece)
                    src[...] = total.astype(src.dtype)
                    copy.start()
                    sends.append(copy)
                    yield
        def final(piece):
            total = summed(w, 0, piece)
            for direction in range(2):
                _, arrived, copy = hop(w, direction, 1, piece)
                copy.wait_recv()
                total = total + arrived[...].astype(jnp.float32)
            return total
        x_out[w] = final(1)
        copy = remote(x_out.at[w], x_in.at[w], xsend.at[w], xrecv.at[w], place.across)
        copy.start()
        sends.append(copy)
        yield
        total = final(0)
        copy.wait_recv()
        out = (o1, o2)[w]
        out[...] = own[w].astype(jnp.float32) - own[2 + w].astype(jnp.float32) * (total + x_in[w])
        yield

    lay(1, g2)
    pair(1)
    lay(0, g1)
    pair(0)
    for _ in scatter(1):
        pass
    for _ in scatter(0):
        pass
    for copy in sends:
        copy.wait_send()


def reduce(grad1, grad2, own):
    f32, bf16 = jnp.float32, jnp.bfloat16
    dma = pltpu.SemaphoreType.DMA
    vmem = pl.BlockSpec(memory_space=pltpu.VMEM)
    block = (ROWS, C)
    return pl.pallas_call(
        reduce_kernel,
        out_shape=(jax.ShapeDtypeStruct(block, f32),) * 2,
        in_specs=[vmem] * 3,
        out_specs=(vmem,) * 2,
        scratch_shapes=[
            pltpu.VMEM((2, NX, NZ, NC) + block, f32),
            pltpu.VMEM((2, NZ, 2) + block, f32),
            pltpu.VMEM((2, NZ, 2) + block, f32),
            pltpu.VMEM((2, 2, 3, 2) + block, bf16),
            pltpu.VMEM((2, 2, 3, 2) + block, bf16),
            pltpu.VMEM((2, 2, 2) + block, f32),
            pltpu.VMEM((2, 2, 2) + block, f32),
            pltpu.VMEM((2,) + block, f32),
            pltpu.VMEM((2,) + block, f32),
            dma((2, NZ, 2)),
            dma((2, NZ, 2)),
            dma((2, 2, 5, 2)),
            dma((2, 2, 5, 2)),
            dma((2,)),
            dma((2,)),
        ],
        compiler_params=pltpu.CompilerParams(
            collective_id=1, has_side_effects=True, vmem_limit_bytes=56 << 20
        ),
        name="reduce_gradients",
    )(grad1, grad2, own)


def time_bias(step_index, ident, subject_table, time_proj):
    half_width = subject_table.shape[1] // 2
    freqs = jnp.exp(-math.log(10000.0) * jnp.arange(half_width, dtype=jnp.float32) / half_width)
    angles = step_index.astype(jnp.float32) * freqs
    embedding = jnp.concatenate([jnp.cos(angles), jnp.sin(angles)])
    onehot = (jnp.arange(subject_table.shape[0], dtype=jnp.int32) == ident).astype(jnp.float32)
    embedding = embedding + jnp.dot(onehot, subject_table, precision=lax.Precision.HIGHEST)
    activated = jax.nn.silu(embedding).astype(jnp.bfloat16)
    return jnp.dot(activated[None, :], time_proj, preferred_element_type=jnp.float32)[0]


def group_norm(values):
    channels = values.shape[2]
    per_group = channels // GN_GROUPS
    counted = values.shape[0] * values.shape[1] * per_group

    def spread(sums):
        return jnp.repeat(sums.reshape(GN_GROUPS, per_group).sum(axis=1) / counted, per_group)

    centre = spread(values.sum(axis=(0, 1)))
    centred = values - centre
    variance = spread((centred * centred).sum(axis=(0, 1)))
    return centred * lax.rsqrt(variance + 1e-05)


def activate(values):
    return jax.nn.silu(group_norm(values))


def stack_taps(act_values):
    frames, points, channels = act_values.shape
    blank = jnp.zeros((1, points, channels), act_values.dtype)
    before = jnp.concatenate([blank, act_values[:-1]], axis=0)
    after = jnp.concatenate([act_values[1:], blank], axis=0)
    return jnp.concatenate([before, act_values, after], axis=2).reshape(
        frames * points, 3 * channels
    )


def fold_taps(grad_rows, frames, points, channels):
    shaped = grad_rows.reshape(frames, points, 3 * channels)
    blank = jnp.zeros((1, points, channels), jnp.float32)
    from_before = jnp.concatenate([shaped[1:, :, :channels], blank], axis=0)
    from_after = jnp.concatenate([blank, shaped[:-1, :, 2 * channels :]], axis=0)
    return shaped[:, :, channels : 2 * channels] + from_before + from_after


def fold_rows(stacked, portion):
    return jnp.dot(stacked, portion, preferred_element_type=jnp.float32)


def grad_terms(stacked, cotangent, weight_scale):
    product = lax.dot_general(
        stacked, cotangent, (((0,), (0,)), ((), ())), preferred_element_type=jnp.float32
    )
    return weight_scale * product


def shards(
    clips,
    targets,
    timestep,
    identity,
    conv1_weight,
    conv2_weight,
    rate1,
    rate2,
    time_proj,
    subject_table,
):
    frames, points, channels = (clips.shape[1], clips.shape[2], clips.shape[3])
    weight_scale = 1.0 / math.sqrt(3 * channels)
    latent = clips[0].astype(jnp.float32)
    bias_row = time_bias(timestep[0], identity[0], subject_table, time_proj)
    stacked_one = stack_taps(activate(latent).astype(jnp.bfloat16))
    contract_last = (((1,), (1,)), ((), ()))
    full_one, full_two, own = gather(conv1_weight, conv2_weight, rate1, rate2)
    mixed_one = fold_rows(stacked_one, full_one)
    hidden = (weight_scale * mixed_one + bias_row).reshape(frames, points, channels)
    act_two, backward = jax.vjp(activate, hidden)
    stacked_two = stack_taps(act_two.astype(jnp.bfloat16))
    mixed_two = fold_rows(stacked_two, full_two)
    output = latent + (weight_scale * mixed_two).reshape(frames, points, channels)
    error = (
        (output - targets[0].astype(jnp.float32))
        .reshape(frames * points, channels)
        .astype(jnp.bfloat16)
    )
    grad_two = grad_terms(stacked_two, error, weight_scale)
    back_rows = lax.dot_general(
        error,
        full_two,
        contract_last,
        preferred_element_type=jnp.float32,
    )
    grad_act = fold_taps(weight_scale * back_rows, frames, points, channels)
    grad_hidden = backward(grad_act)[0].reshape(frames * points, channels).astype(jnp.bfloat16)
    grad_one = grad_terms(stacked_one, grad_hidden, weight_scale)
    adapted_one, adapted_two = reduce(grad_one, grad_two, own)
    return (adapted_one[None], adapted_two[None])


def solution(mesh):
    return jax.shard_map(
        shards,
        mesh=mesh,
        in_specs=(
            P(("group", "member"), None, None, None),
            P(("group", "member"), None, None, None),
            P(("group", "member")),
            P(("group", "member")),
            P("member", "group"),
            P("member", "group"),
            P("member", "group"),
            P("member", "group"),
            P(),
            P(),
        ),
        out_specs=(P("group", "member", None), P("group", "member", None)),
        check_vma=False,
    )
```

```python
import functools
import math

import jax
import jax.numpy as jnp
from jax import lax
from jax.experimental import pallas as pl
from jax.experimental.pallas import tpu as pltpu
from jax.sharding import PartitionSpec as P

GN_GROUPS = 32
MESH = pl.DeviceIdType.MESH
N_GROUP, N_MEMBER, NZ, NC, NX = 8, 32, 8, 2, 2
ROWS, COLS, C = 60, 80, 640
TAPS = 3 * C
FRAMES, HW = 14, 64
POINTS = FRAMES * HW
PER_GROUP = C // GN_GROUPS
SCALE = 1.0 / math.sqrt(TAPS)
UNIT = 128


class Place:
    def __init__(self):
        self.g = lax.axis_index("group")
        self.m = lax.axis_index("member")
        self.core = lax.rem(self.m, 2)
        self.q = lax.div(self.m, 2)
        self.z = lax.rem(self.q, NZ)
        self.xh = lax.div(self.q, NZ)
        self.up = self.at(self.xh, self.zof(1), self.core)
        self.down = self.at(self.xh, self.zof(-1), self.core)
        self.across = self.at(1 - self.xh, self.z, self.core)
        self.sibling = self.at(self.xh, self.z, 1 - self.core)

    def at(self, xh, z, core):
        return (self.g, (xh * NZ + z) * 2 + core)

    def zof(self, step):
        return lax.rem(self.z + (step + NZ), NZ)

    def peer(self, step):
        return lax.rem(self.g + step, N_GROUP)

    def xof(self, piece):
        return self.xh if piece == 0 else 1 - self.xh


def remote(src, dst, send, recv, device):
    return pltpu.make_async_remote_copy(
        src_ref=src, dst_ref=dst, send_sem=send, recv_sem=recv, device_id=device, device_id_type=MESH
    )


def enter(place, with_group):
    barrier = pltpu.get_barrier_semaphore()
    partners = [place.up, place.down, place.across, place.sibling]
    if with_group:
        partners += [(place.peer(step), place.m) for step in range(1, N_GROUP)]
    for partner in partners:
        pl.semaphore_signal(barrier, inc=1, device_id=partner, device_id_type=MESH)
    pl.semaphore_wait(barrier, len(partners))


def exists(direction, dist, piece):
    return dist < 4 or (dist == 4 and piece == direction)


def step_kernel(
    clip_hbm, target_hbm, proj_hbm, embed, w1, w2, r1, r2, o1, o2,
    clip, target, proj, same_group, act_one, act_two, err, grad_hid, flip_one, flip_two, hid, weights, grad,
    gbuf, wbuf, own, blocks, sib_in, hop_out, hop_in, last_out, last_in, x_out, x_in,
    load_sem, gsend, grecv, zsend, zrecv, xsend, xrecv, ssend, srecv,
    rsend, rrecv, ysend, yrecv, psend, precv,
):
    f32, bf16 = jnp.float32, jnp.bfloat16
    place = Place()
    sends = []

    def go(copy):
        copy.start()
        sends.append(copy)

    loads = [
        pltpu.make_async_copy(src, dst, load_sem.at[i])
        for i, (src, dst) in enumerate(((clip_hbm, clip), (proj_hbm, proj), (target_hbm, target)))
    ]
    for load in loads:
        load.start()
    for index, ref in enumerate((w1, w2, r1, r2)):
        gbuf[index, place.g] = ref[...]
    enter(place, True)

    def group_copy(part, step, here):
        block = pl.ds(part, 1) if part < 2 else pl.ds(2, 2)
        source = place.g if here else lax.rem(place.g + (N_GROUP - step), N_GROUP)
        ref = gbuf.at[block, source]
        return remote(ref, ref, gsend.at[part, step], grecv.at[part, step], (place.peer(step), place.m))

    for part in range(3):
        for step in range(1, N_GROUP):
            go(group_copy(part, step, True))

    def assemble(index):
        parts = [gbuf[index, group].astype(f32) for group in range(N_GROUP)]
        return jnp.concatenate(parts, axis=1).astype(bf16)

    def slot(w, dist, piece):
        return wbuf.at[w, place.xof(piece), place.zof(-dist), place.core]

    def share(w, dist, piece):
        ref = slot(w, dist, piece)
        go(remote(ref, ref, ssend.at[w, dist % NZ, piece], srecv.at[w, dist % NZ, piece], place.sibling))

    def ring_copy(w, direction, dist, piece, here):
        sign = 1 if direction == 0 else -1
        ref = slot(w, sign * (dist - 1 if here else dist), piece)
        to = place.up if direction == 0 else place.down
        return remote(ref, ref, zsend.at[w, direction, dist, piece], zrecv.at[w, direction, dist, piece], to)

    def forward(w, direction, dist, piece):
        if exists(direction, dist, piece):
            go(ring_copy(w, direction, dist, piece, True))

    def ring_start(w):
        for step in range(1, N_GROUP):
            group_copy(w, step, False).wait_recv()
        whole = assemble(w)
        own[w] = whole
        wbuf[w, place.xh, place.z, place.core] = whole
        mine = slot(w, 0, 0)
        go(remote(mine, mine, xsend.at[w], xrecv.at[w], place.across))

    def ring(w):
        for direction in range(2):
            forward(w, direction, 1, 0)
        share(w, 0, 0)
        yield
        theirs = slot(w, 0, 1)
        remote(theirs, theirs, xsend.at[w], xrecv.at[w], place.across).wait_recv()
        for direction in range(2):
            forward(w, direction, 1, 1)
        share(w, 0, 1)
        yield
        for dist in range(1, 5):
            for piece in range(2):
                for direction in range(2):
                    if exists(direction, dist, piece):
                        ring_copy(w, direction, dist, piece, False).wait_recv()
                        forward(w, direction, dist + 1, piece)
                        share(w, dist if direction == 0 else -dist, piece)
                        yield

    def dense(w):
        for dist in range(NZ):
            for piece in range(2):
                ref = wbuf.at[w, place.xof(piece), place.zof(-dist), 1 - place.core]
                remote(ref, ref, ssend.at[w, dist, piece], srecv.at[w, dist, piece], place.sibling).wait_recv()
        for m in range(N_MEMBER):
            weights[w, ROWS * m : ROWS * (m + 1), :] = wbuf[w, m // 16, (m // 2) % NZ, m % 2]

    def lay(w):
        for m in range(N_MEMBER):
            blocks[w, m // 16, (m // 2) % NZ, m % 2] = grad[ROWS * m : ROWS * (m + 1), :]

    def pair_copy(w, dist, piece):
        src = blocks.at[w, place.xof(piece), place.zof(dist), 1 - place.core]
        dst = sib_in.at[w, dist, piece]
        return remote(src, dst, psend.at[w, dist, piece], precv.at[w, dist, piece], place.sibling)

    def pair(w):
        for dist in (4, 3, 5, 2, 6, 1, 7, 0):
            for piece in range(2):
                go(pair_copy(w, dist, piece))

    def summed(w, dist, piece):
        pair_copy(w, dist, piece).wait_recv()
        return blocks[w, place.xof(piece), place.zof(dist), place.core] + sib_in[w, dist, piece]

    def hop(w, direction, dist, piece):
        to = place.up if direction == 0 else place.down
        if dist == 1:
            src, dst = last_out.at[w, direction, piece], last_in.at[w, direction, piece]
        else:
            src, dst = hop_out.at[w, direction, dist - 2, piece], hop_in.at[w, direction, dist - 2, piece]
        return src, dst, remote(src, dst, rsend.at[w, direction, dist, piece], rrecv.at[w, direction, dist, piece], to)

    def scatter(w):
        for dist in (4, 3, 2, 1):
            for piece in range(2):
                for direction in range(2):
                    if not exists(direction, dist, piece):
                        continue
                    total = summed(w, dist if direction == 0 else NZ - dist, piece)
                    if exists(direction, dist + 1, piece):
                        _, arrived, copy = hop(w, direction, dist + 1, piece)
                        copy.wait_recv()
                        total = total + arrived[...].astype(f32)
                    src, _, copy = hop(w, direction, dist, piece)
                    src[...] = total.astype(src.dtype)
                    go(copy)
                    yield

        def final(piece):
            total = summed(w, 0, piece)
            for direction in range(2):
                _, arrived, copy = hop(w, direction, 1, piece)
                copy.wait_recv()
                total = total + arrived[...]
            return total

        x_out[w] = final(1)
        copy = remote(x_out.at[w], x_in.at[w], ysend.at[w], yrecv.at[w], place.across)
        go(copy)
        yield
        total = final(0)
        copy.wait_recv()
        out = (o1, o2)[w]
        out[...] = own[w].astype(f32) - own[2 + w].astype(f32) * (SCALE * (total + x_in[w]))
        yield

    def rows(index, size=UNIT):
        return pl.ds(index * size, size)

    def fold(values):
        return values.reshape(values.shape[0] // 8, 8, C).sum(axis=0)

    def spread(sums):
        column = sums.sum(axis=0, keepdims=True)
        top = column.astype(bf16)
        rest = column - top.astype(f32)
        middle = rest.astype(bf16)
        low = (rest - middle.astype(f32)).astype(bf16)
        terms = jnp.concatenate([top, middle, low, jnp.zeros((13, C), bf16)], axis=0)
        total = jnp.dot(terms, same_group[...], preferred_element_type=f32)
        return total.sum(axis=0, keepdims=True) * (1.0 / (POINTS * PER_GROUP))

    def sweep(body, start):
        return lax.fori_loop(0, FRAMES, lambda i, carry: body(pl.ds(pl.multiple_of(i * HW, HW), HW), carry), start)

    def padded(i):
        return pl.ds(HW + i * UNIT, UNIT)

    def silu(v):
        return v / (1.0 + jnp.exp(-v))

    first = lax.broadcasted_iota(jnp.int32, (C, C), 0)
    second = lax.broadcasted_iota(jnp.int32, (C, C), 1)
    same_group[...] = (((first * 3277) >> 16) == ((second * 3277) >> 16)).astype(f32).astype(bf16)
    blank = jnp.zeros((HW, C), bf16)
    for ref in (act_one, act_two, err, grad_hid):
        ref[0:HW, :] = blank
        ref[HW + POINTS :, :] = blank
    zero = jnp.zeros((8, C), f32)
    loads[0].wait()
    centre = spread(sweep(lambda at, acc: acc + fold(clip[at, :].astype(f32)), zero))

    def squares(ref, mean):
        def body(at, acc):
            off = ref[at, :].astype(f32) - mean
            return acc + fold(off * off)

        return lax.rsqrt(spread(sweep(body, zero)) + 1e-05)

    ring_start(0)
    ring_one = ring(0)
    next(ring_one)
    inverse = squares(clip, centre)
    next(ring_one)
    units = POINTS // UNIT
    for i in range(units):
        values = (clip[rows(i), :].astype(f32) - centre) * inverse
        act_one[padded(i), :] = silu(values).astype(bf16)
        next(ring_one)
    loads[1].wait()
    bias = jnp.dot(embed[...], proj[...], preferred_element_type=f32)[0:1]
    ring_start(1)
    ring_two = ring(1)
    for i in range(units):
        flip_one[:, rows(i)] = act_one[padded(i), :].T
        next(ring_one, None)
    for _ in ring_one:
        pass
    next(ring_two)
    dense(0)

    def stacked(ref, start, size, taps):
        return jnp.concatenate([ref[pl.ds(start + HW * tap, size), :] for tap in taps], axis=1)

    half = POINTS // 2
    sums = zero
    for part in range(2):
        mixed = jnp.dot(stacked(act_one, part * half, half, (0, 1, 2)), weights[0], preferred_element_type=f32)
        values = SCALE * mixed + bias
        hid[pl.ds(part * half, half), :] = values
        sums = sums + fold(values)
        for _ in range(3):
            next(ring_two)
    centre_two = spread(sums)
    inverse_two = squares(hid, centre_two)
    next(ring_two)
    for i in range(units):
        values = (hid[rows(i), :] - centre_two) * inverse_two
        hid[rows(i), :] = values
        act_two[padded(i), :] = silu(values).astype(bf16)
        next(ring_two, None)
    for i in range(units):
        flip_two[:, rows(i)] = act_two[padded(i), :].T
        next(ring_two, None)
    for _ in ring_two:
        pass
    dense(1)
    loads[2].wait()

    for part in range(2):
        at = pl.ds(part * half, half)
        mixed = jnp.dot(stacked(act_two, part * half, half, (0, 1, 2)), weights[1], preferred_element_type=f32)
        output = clip[at, :].astype(f32) + SCALE * mixed
        err[pl.ds(HW + part * half, half), :] = (output - target[at, :].astype(f32)).astype(bf16)

    def weight_grad(flipped, ref, tap):
        grad[C * tap : C * (tap + 1), :] = jnp.dot(
            flipped[...], ref[pl.ds(HW * (2 - tap), POINTS), :], preferred_element_type=f32
        )

    for tap in range(3):
        weight_grad(flip_two, err, tap)
    lay(1)
    pair(1)

    scatter_two = scatter(1)
    sum_grad, sum_mixed = zero, zero
    for part in range(2):
        at = pl.ds(part * half, half)
        back = jnp.zeros((half, C), f32)
        for tap in range(3):
            back = back + lax.dot_general(
                err[pl.ds(part * half + HW * (2 - tap), half), :],
                weights[1, C * tap : C * (tap + 1), :],
                (((1,), (1,)), ((), ())),
                preferred_element_type=f32,
            )
        values = hid[at, :]
        gate = 1.0 / (1.0 + jnp.exp(-values))
        inner = (SCALE * back) * (gate * (1.0 + values * (1.0 - gate)))
        grad[at, :] = inner
        sum_grad = sum_grad + fold(inner)
        sum_mixed = sum_mixed + fold(inner * values)
        for _ in range(4):
            next(scatter_two)
    mean_grad, mean_mixed = spread(sum_grad), spread(sum_mixed)
    for i in range(units):
        inner = grad[rows(i), :] - mean_grad - hid[rows(i), :] * mean_mixed
        grad_hid[padded(i), :] = (inner * inverse_two).astype(bf16)
        if i % 2:
            next(scatter_two)
    for tap in range(3):
        weight_grad(flip_one, grad_hid, tap)
        next(scatter_two)
    lay(0)
    pair(0)
    for step in range(1, N_GROUP):
        group_copy(2, step, False).wait_recv()
    own[2] = assemble(2)
    own[3] = assemble(3)
    scatter_one = scatter(0)
    for _ in scatter_two:
        next(scatter_one, None)
    for _ in scatter_one:
        pass
    for copy in sends:
        copy.wait_send()


def step(clip, target, time_proj, embed, w1, w2, r1, r2):
    f32, bf16 = jnp.float32, jnp.bfloat16
    dma = pltpu.SemaphoreType.DMA
    vmem = pl.BlockSpec(memory_space=pltpu.VMEM)
    anywhere = pl.BlockSpec(memory_space=pl.ANY)
    block = (ROWS, C)
    wide = (POINTS + 2 * HW, C)
    return pl.pallas_call(
        step_kernel,
        out_shape=(jax.ShapeDtypeStruct(block, f32),) * 2,
        in_specs=[anywhere] * 3 + [vmem] * 5,
        out_specs=(vmem,) * 2,
        scratch_shapes=[
            pltpu.VMEM((POINTS, C), bf16),
            pltpu.VMEM((POINTS, C), bf16),
            pltpu.VMEM(time_proj.shape, bf16),
            pltpu.VMEM((C, C), bf16),
            pltpu.VMEM(wide, bf16),
            pltpu.VMEM(wide, bf16),
            pltpu.VMEM(wide, bf16),
            pltpu.VMEM(wide, bf16),
            pltpu.VMEM((C, POINTS), bf16),
            pltpu.VMEM((C, POINTS), bf16),
            pltpu.VMEM((POINTS, C), f32),
            pltpu.VMEM((2, TAPS, C), bf16),
            pltpu.VMEM((TAPS, C), f32),
            pltpu.VMEM((4, N_GROUP, ROWS, COLS), bf16),
            pltpu.VMEM((2, NX, NZ, NC) + block, bf16),
            pltpu.VMEM((4,) + block, bf16),
            pltpu.VMEM((2, NX, NZ, NC) + block, f32),
            pltpu.VMEM((2, NZ, 2) + block, f32),
            pltpu.VMEM((2, 2, 3, 2) + block, bf16),
            pltpu.VMEM((2, 2, 3, 2) + block, bf16),
            pltpu.VMEM((2, 2, 2) + block, f32),
            pltpu.VMEM((2, 2, 2) + block, f32),
            pltpu.VMEM((2,) + block, f32),
            pltpu.VMEM((2,) + block, f32),
            dma((3,)),
            dma((3, N_GROUP)),
            dma((3, N_GROUP)),
            dma((2, 2, 5, 2)),
            dma((2, 2, 5, 2)),
            dma((2,)),
            dma((2,)),
            dma((2, NZ, 2)),
            dma((2, NZ, 2)),
            dma((2, 2, 5, 2)),
            dma((2, 2, 5, 2)),
            dma((2,)),
            dma((2,)),
            dma((2, NZ, 2)),
            dma((2, NZ, 2)),
        ],
        compiler_params=pltpu.CompilerParams(
            collective_id=0, has_side_effects=True, vmem_limit_bytes=62 << 20
        ),
        name="inner_step",
    )(clip, target, time_proj, embed, w1, w2, r1, r2)


def embed_rows(step_index, ident, subject_table):
    half_width = subject_table.shape[1] // 2
    freqs = jnp.exp(-math.log(10000.0) * jnp.arange(half_width, dtype=jnp.float32) / half_width)
    angles = step_index.astype(jnp.float32) * freqs
    embedding = jnp.concatenate([jnp.cos(angles), jnp.sin(angles)])
    onehot = (jnp.arange(subject_table.shape[0], dtype=jnp.int32) == ident).astype(jnp.float32)
    embedding = embedding + jnp.dot(onehot, subject_table, precision=lax.Precision.HIGHEST)
    activated = jax.nn.silu(embedding).astype(jnp.bfloat16)
    return jnp.broadcast_to(activated[None, :], (16, activated.shape[0]))


def shards(
    clips,
    targets,
    timestep,
    identity,
    conv1_weight,
    conv2_weight,
    rate1,
    rate2,
    time_proj,
    subject_table,
):
    embed = embed_rows(timestep[0], identity[0], subject_table)
    adapted_one, adapted_two = step(
        clips.reshape(POINTS, C),
        targets.reshape(POINTS, C),
        time_proj,
        embed,
        conv1_weight,
        conv2_weight,
        rate1,
        rate2,
    )
    return (adapted_one[None], adapted_two[None])


def solution(mesh):
    return jax.shard_map(
        shards,
        mesh=mesh,
        in_specs=(
            P(("group", "member"), None, None, None),
            P(("group", "member"), None, None, None),
            P(("group", "member")),
            P(("group", "member")),
            P("member", "group"),
            P("member", "group"),
            P("member", "group"),
            P("member", "group"),
            P(),
            P(),
        ),
        out_specs=(P("group", "member", None), P("group", "member", None)),
        check_vma=False,
    )
```

```python
import functools
import math

import jax
import jax.numpy as jnp
from jax import lax
from jax.experimental import pallas as pl
from jax.experimental.pallas import tpu as pltpu
from jax.sharding import PartitionSpec as P

GN_GROUPS = 32
MESH = pl.DeviceIdType.MESH
N_GROUP, N_MEMBER, NZ, NC, NX = 8, 32, 8, 2, 2
ROWS, COLS, C = 60, 80, 640
TAPS = 3 * C
FRAMES, HW = 14, 64
POINTS = FRAMES * HW
PER_GROUP = C // GN_GROUPS
SCALE = 1.0 / math.sqrt(TAPS)
UNIT = 128


class Place:
    def __init__(self):
        self.g = lax.axis_index("group")
        self.m = lax.axis_index("member")
        self.core = lax.rem(self.m, 2)
        self.q = lax.div(self.m, 2)
        self.z = lax.rem(self.q, NZ)
        self.xh = lax.div(self.q, NZ)
        self.up = self.at(self.xh, self.zof(1), self.core)
        self.down = self.at(self.xh, self.zof(-1), self.core)
        self.across = self.at(1 - self.xh, self.z, self.core)
        self.sibling = self.at(self.xh, self.z, 1 - self.core)
        self.x_lo = lax.rem(self.g, 2)
        self.y_lo = lax.rem(lax.div(self.g, 2), 2)
        self.beside_x = (self.g + 1 - 2 * self.x_lo, self.m)
        self.beside_y = (self.g + 2 - 4 * self.y_lo, self.m)

    def at(self, xh, z, core):
        return (self.g, (xh * NZ + z) * 2 + core)

    def zof(self, step):
        return lax.rem(self.z + (step + NZ), NZ)

    def peer(self, step):
        return lax.rem(self.g + step, N_GROUP)

    def xof(self, piece):
        return self.xh if piece == 0 else 1 - self.xh


def remote(src, dst, send, recv, device):
    return pltpu.make_async_remote_copy(
        src_ref=src, dst_ref=dst, send_sem=send, recv_sem=recv, device_id=device, device_id_type=MESH
    )


def enter(place, with_group):
    barrier = pltpu.get_barrier_semaphore()
    partners = [place.up, place.down, place.across, place.sibling]
    if with_group:
        partners += [(place.peer(step), place.m) for step in range(1, N_GROUP)]
    for partner in partners:
        pl.semaphore_signal(barrier, inc=1, device_id=partner, device_id_type=MESH)
    pl.semaphore_wait(barrier, len(partners))


def exists(direction, dist, piece):
    return dist < 4 or (dist == 4 and piece == direction)


def step_kernel(
    clip_hbm, target_hbm, proj_hbm, embed, w1, w2, r1, r2, o1, o2,
    clip, target, proj, same_group, act_one, act_two, err, grad_hid, flip_one, flip_two, hid, weights, grad,
    gbuf, wbuf, own, blocks, sib_in, hop_out, hop_in, last_out, last_in, x_out, x_in,
    load_sem, gsend, grecv, zsend, zrecv, xsend, xrecv, ssend, srecv, bsend, brecv,
    rsend, rrecv, ysend, yrecv, psend, precv,
):
    f32, bf16 = jnp.float32, jnp.bfloat16
    place = Place()
    sends = []

    def go(copy):
        copy.start()
        sends.append(copy)

    loads = [
        pltpu.make_async_copy(src, dst, load_sem.at[i])
        for i, (src, dst) in enumerate(((clip_hbm, clip), (proj_hbm, proj), (target_hbm, target)))
    ]
    for load in loads:
        load.start()
    for index, ref in enumerate((w1, w2, r1, r2)):
        gbuf[index, place.g] = ref[...]
    enter(place, True)

    def group_copy(part, step, here):
        block = pl.ds(part, 1) if part < 2 else pl.ds(2, 2)
        source = place.g if here else lax.rem(place.g + (N_GROUP - step), N_GROUP)
        ref = gbuf.at[block, source]
        return remote(ref, ref, gsend.at[part, step], grecv.at[part, step], (place.peer(step), place.m))

    def group_send(part):
        for step in range(1, N_GROUP):
            go(group_copy(part, step, True))

    group_send(0)
    group_send(1)

    def assemble(index):
        parts = [gbuf[index, group].astype(f32) for group in range(N_GROUP)]
        return jnp.concatenate(parts, axis=1)

    tile_slot = (2 * place.x_lo, 2 - 2 * place.x_lo, 1 + 2 * place.y_lo, 3 - 2 * place.y_lo)

    def slot(w, dist, piece, first, count, core=None):
        core = place.core if core is None else core
        return wbuf.at[w, place.xof(piece), place.zof(-dist), core, pl.ds(first, count)]

    def share_copy(w, dist, piece, high, count, here):
        ref = slot(w, dist, piece, 2 * high, count, place.core if here else 1 - place.core)
        at = (w, high, dist % NZ, piece)
        return remote(ref, ref, ssend.at[at], srecv.at[at], place.sibling)

    def side_copy(w, side, dist, piece):
        src, dst = slot(w, dist, piece, side, 1), slot(w, dist, piece, side + 2, 1)
        at = (w, side, dist % NZ, piece)
        return remote(src, dst, bsend.at[at], brecv.at[at], (place.beside_x, place.beside_y)[side])

    def ring_copy(w, direction, dist, piece, here):
        sign = 1 if direction == 0 else -1
        ref = slot(w, sign * (dist - 1 if here else dist), piece, 0, 2)
        to = place.up if direction == 0 else place.down
        return remote(ref, ref, zsend.at[w, direction, dist, piece], zrecv.at[w, direction, dist, piece], to)

    def forward(w, direction, dist, piece):
        if exists(direction, dist, piece):
            go(ring_copy(w, direction, dist, piece, True))

    def hand_on(w, dist, piece):
        for side in range(2):
            go(side_copy(w, side, dist, piece))
        go(share_copy(w, dist, piece, 0, 2, True))

    def across_copy(w, piece):
        ref = slot(w, 0, piece, 0, 2)
        return remote(ref, ref, xsend.at[w], xrecv.at[w], place.across)

    def ring_start(w):
        for step in range(1, N_GROUP):
            group_copy(w, step, False).wait_recv()
        whole = jnp.concatenate([assemble(w), jnp.zeros((4, C), f32)], axis=0).astype(bf16)
        own[w] = whole[0:ROWS]
        for tile in range(4):
            wbuf[w, place.xh, place.z, place.core, tile_slot[tile]] = whole[16 * tile : 16 * (tile + 1)]
        go(across_copy(w, 0))
        for direction in range(2):
            forward(w, direction, 1, 0)
        go(share_copy(w, 0, 0, 0, 4, True))

    def ring_across(w):
        across_copy(w, 1).wait_recv()
        for direction in range(2):
            forward(w, direction, 1, 1)
        hand_on(w, 0, 1)

    def ring_step(w, dist):
        for piece in range(2):
            for direction in range(2):
                if exists(direction, dist, piece):
                    ring_copy(w, direction, dist, piece, False).wait_recv()
                    forward(w, direction, dist + 1, piece)
                    hand_on(w, dist if direction == 0 else -dist, piece)

    def ring_sides(w, dist):
        for piece in range(2):
            for direction in range(2):
                far = dist if direction == 0 else -dist
                if not exists(direction, dist, piece) or dist == 0 and (direction == 1 or piece == 0):
                    continue
                for side in range(2):
                    side_copy(w, side, far, piece).wait_recv()
                go(share_copy(w, far, piece, 1, 2, True))

    def dense(w):
        for dist in range(NZ):
            for piece in range(2):
                if (dist, piece) == (0, 0):
                    share_copy(w, dist, piece, 0, 4, False).wait_recv()
                else:
                    share_copy(w, dist, piece, 0, 2, False).wait_recv()
                    share_copy(w, dist, piece, 1, 2, False).wait_recv()
        for m in range(N_MEMBER):
            for tile in range(4):
                start, size = ROWS * m + 16 * tile, min(16, ROWS - 16 * tile)
                block = wbuf[w, m // 16, (m // 2) % NZ, m % 2, tile_slot[tile]]
                weights[w, start : start + size, :] = block[0:size]

    def lay(w):
        for m in range(N_MEMBER):
            blocks[w, m // 16, (m // 2) % NZ, m % 2] = grad[ROWS * m : ROWS * (m + 1), :]

    def pair_copy(w, dist, piece):
        src = blocks.at[w, place.xof(piece), place.zof(dist), 1 - place.core]
        dst = sib_in.at[w, dist, piece]
        return remote(src, dst, psend.at[w, dist, piece], precv.at[w, dist, piece], place.sibling)

    def pair(w):
        for dist in (4, 3, 5, 2, 6, 1, 7, 0):
            for piece in range(2):
                go(pair_copy(w, dist, piece))

    def summed(w, dist, piece):
        pair_copy(w, dist, piece).wait_recv()
        return blocks[w, place.xof(piece), place.zof(dist), place.core] + sib_in[w, dist, piece]

    def hop(w, direction, dist, piece):
        to = place.up if direction == 0 else place.down
        if dist == 1:
            src, dst = last_out.at[w, direction, piece], last_in.at[w, direction, piece]
        else:
            src, dst = hop_out.at[w, direction, dist - 2, piece], hop_in.at[w, direction, dist - 2, piece]
        return src, dst, remote(src, dst, rsend.at[w, direction, dist, piece], rrecv.at[w, direction, dist, piece], to)

    def scatter(w):
        for dist in (4, 3, 2, 1):
            for piece in range(2):
                for direction in range(2):
                    if not exists(direction, dist, piece):
                        continue
                    total = summed(w, dist if direction == 0 else NZ - dist, piece)
                    if exists(direction, dist + 1, piece):
                        _, arrived, copy = hop(w, direction, dist + 1, piece)
                        copy.wait_recv()
                        total = total + arrived[...].astype(f32)
                    src, _, copy = hop(w, direction, dist, piece)
                    src[...] = total.astype(src.dtype)
                    go(copy)
                    yield

        def final(piece):
            total = summed(w, 0, piece)
            for direction in range(2):
                _, arrived, copy = hop(w, direction, 1, piece)
                copy.wait_recv()
                total = total + arrived[...]
            return total

        x_out[w] = final(1)
        copy = remote(x_out.at[w], x_in.at[w], ysend.at[w], yrecv.at[w], place.across)
        go(copy)
        yield
        total = final(0)
        copy.wait_recv()
        out = (o1, o2)[w]
        out[...] = own[w].astype(f32) - own[2 + w].astype(f32) * (SCALE * (total + x_in[w]))
        yield

    def rows(index, size=UNIT):
        return pl.ds(index * size, size)

    def fold(values):
        return values.reshape(values.shape[0] // 8, 8, C).sum(axis=0)

    def spread(sums):
        column = sums.sum(axis=0, keepdims=True)
        top = column.astype(bf16)
        rest = column - top.astype(f32)
        middle = rest.astype(bf16)
        low = (rest - middle.astype(f32)).astype(bf16)
        terms = jnp.concatenate([top, middle, low, jnp.zeros((13, C), bf16)], axis=0)
        total = jnp.dot(terms, same_group[...], preferred_element_type=f32)
        return total.sum(axis=0, keepdims=True) * (1.0 / (POINTS * PER_GROUP))

    def sweep(body, start):
        return lax.fori_loop(0, FRAMES, lambda i, carry: body(pl.ds(pl.multiple_of(i * HW, HW), HW), carry), start)

    def padded(i):
        return pl.ds(HW + i * UNIT, UNIT)

    def silu(v):
        return v / (1.0 + jnp.exp(-v))

    first = lax.broadcasted_iota(jnp.int32, (C, C), 0)
    second = lax.broadcasted_iota(jnp.int32, (C, C), 1)
    same_group[...] = (((first * 3277) >> 16) == ((second * 3277) >> 16)).astype(f32).astype(bf16)
    blank = jnp.zeros((HW, C), bf16)
    for ref in (act_one, act_two, err, grad_hid):
        ref[0:HW, :] = blank
        ref[HW + POINTS :, :] = blank
    zero = jnp.zeros((8, C), f32)
    loads[0].wait()
    centre = spread(sweep(lambda at, acc: acc + fold(clip[at, :].astype(f32)), zero))

    def squares(ref, mean):
        def body(at, acc):
            off = ref[at, :].astype(f32) - mean
            return acc + fold(off * off)

        return lax.rsqrt(spread(sweep(body, zero)) + 1e-05)

    inverse = squares(clip, centre)
    units = POINTS // UNIT

    def act_unit(i):
        values = (clip[rows(i), :].astype(f32) - centre) * inverse
        act_one[padded(i), :] = silu(values).astype(bf16)

    def flip_unit(flipped, ref, i):
        flipped[:, rows(i)] = ref[padded(i), :].T

    ring_start(0)
    act_unit(0)
    act_unit(1)
    act_unit(2)
    ring_across(0)
    ring_start(1)
    act_unit(3)
    ring_step(0, 1)
    act_unit(4)
    ring_across(1)
    ring_sides(0, 0)
    act_unit(5)
    ring_step(0, 2)
    ring_step(1, 1)
    act_unit(6)
    ring_sides(0, 1)
    loads[1].wait()
    bias = jnp.dot(embed[...], proj[...], preferred_element_type=f32)[0:1]
    ring_step(0, 3)
    ring_step(1, 2)
    ring_sides(1, 0)
    for i in range(3):
        flip_unit(flip_one, act_one, i)
    ring_sides(0, 2)
    ring_step(0, 4)
    ring_step(1, 3)
    ring_sides(1, 1)
    for i in range(3, units):
        flip_unit(flip_one, act_one, i)
    ring_sides(0, 3)
    ring_sides(0, 4)
    ring_step(1, 4)
    ring_sides(1, 2)
    dense(0)

    def stacked(ref, start, size, taps):
        return jnp.concatenate([ref[pl.ds(start + HW * tap, size), :] for tap in taps], axis=1)

    half = POINTS // 2
    sums = zero
    for part in range(2):
        mixed = jnp.dot(stacked(act_one, part * half, half, (0, 1, 2)), weights[0], preferred_element_type=f32)
        values = SCALE * mixed + bias
        hid[pl.ds(part * half, half), :] = values
        sums = sums + fold(values)
        ring_sides(1, 3 + part)
    group_send(2)
    centre_two = spread(sums)
    inverse_two = squares(hid, centre_two)
    for i in range(units):
        values = (hid[rows(i), :] - centre_two) * inverse_two
        hid[rows(i), :] = values
        act_two[padded(i), :] = silu(values).astype(bf16)
    for i in range(units):
        flip_unit(flip_two, act_two, i)
    dense(1)
    loads[2].wait()

    for part in range(2):
        at = pl.ds(part * half, half)
        mixed = jnp.dot(stacked(act_two, part * half, half, (0, 1, 2)), weights[1], preferred_element_type=f32)
        output = clip[at, :].astype(f32) + SCALE * mixed
        err[pl.ds(HW + part * half, half), :] = (output - target[at, :].astype(f32)).astype(bf16)

    def weight_grad(flipped, ref, tap):
        grad[C * tap : C * (tap + 1), :] = jnp.dot(
            flipped[...], ref[pl.ds(HW * (2 - tap), POINTS), :], preferred_element_type=f32
        )

    for tap in range(3):
        weight_grad(flip_two, err, tap)
    lay(1)
    pair(1)

    scatter_two = scatter(1)
    sum_grad, sum_mixed = zero, zero
    for part in range(2):
        at = pl.ds(part * half, half)
        back = jnp.zeros((half, C), f32)
        for tap in range(3):
            back = back + lax.dot_general(
                err[pl.ds(part * half + HW * (2 - tap), half), :],
                weights[1, C * tap : C * (tap + 1), :],
                (((1,), (1,)), ((), ())),
                preferred_element_type=f32,
            )
        values = hid[at, :]
        gate = 1.0 / (1.0 + jnp.exp(-values))
        inner = (SCALE * back) * (gate * (1.0 + values * (1.0 - gate)))
        grad[at, :] = inner
        sum_grad = sum_grad + fold(inner)
        sum_mixed = sum_mixed + fold(inner * values)
        for _ in range(4):
            next(scatter_two)
    mean_grad, mean_mixed = spread(sum_grad), spread(sum_mixed)
    for i in range(units):
        inner = grad[rows(i), :] - mean_grad - hid[rows(i), :] * mean_mixed
        grad_hid[padded(i), :] = (inner * inverse_two).astype(bf16)
        if i % 2:
            next(scatter_two)
    for tap in range(3):
        weight_grad(flip_one, grad_hid, tap)
        next(scatter_two)
    lay(0)
    pair(0)
    for step in range(1, N_GROUP):
        group_copy(2, step, False).wait_recv()
    own[2] = assemble(2).astype(bf16)
    own[3] = assemble(3).astype(bf16)
    scatter_one = scatter(0)
    for _ in scatter_two:
        next(scatter_one, None)
    for _ in scatter_one:
        pass
    for copy in sends:
        copy.wait_send()


def step(clip, target, time_proj, embed, w1, w2, r1, r2):
    f32, bf16 = jnp.float32, jnp.bfloat16
    dma = pltpu.SemaphoreType.DMA
    vmem = pl.BlockSpec(memory_space=pltpu.VMEM)
    anywhere = pl.BlockSpec(memory_space=pl.ANY)
    block = (ROWS, C)
    wide = (POINTS + 2 * HW, C)
    return pl.pallas_call(
        step_kernel,
        out_shape=(jax.ShapeDtypeStruct(block, f32),) * 2,
        in_specs=[anywhere] * 3 + [vmem] * 5,
        out_specs=(vmem,) * 2,
        scratch_shapes=[
            pltpu.VMEM((POINTS, C), bf16),
            pltpu.VMEM((POINTS, C), bf16),
            pltpu.VMEM(time_proj.shape, bf16),
            pltpu.VMEM((C, C), bf16),
            pltpu.VMEM(wide, bf16),
            pltpu.VMEM(wide, bf16),
            pltpu.VMEM(wide, bf16),
            pltpu.VMEM(wide, bf16),
            pltpu.VMEM((C, POINTS), bf16),
            pltpu.VMEM((C, POINTS), bf16),
            pltpu.VMEM((POINTS, C), f32),
            pltpu.VMEM((2, TAPS, C), bf16),
            pltpu.VMEM((TAPS, C), f32),
            pltpu.VMEM((4, N_GROUP, ROWS, COLS), bf16),
            pltpu.VMEM((2, NX, NZ, NC, 4, 16, C), bf16),
            pltpu.VMEM((4,) + block, bf16),
            pltpu.VMEM((2, NX, NZ, NC) + block, f32),
            pltpu.VMEM((2, NZ, 2) + block, f32),
            pltpu.VMEM((2, 2, 3, 2) + block, bf16),
            pltpu.VMEM((2, 2, 3, 2) + block, bf16),
            pltpu.VMEM((2, 2, 2) + block, f32),
            pltpu.VMEM((2, 2, 2) + block, f32),
            pltpu.VMEM((2,) + block, f32),
            pltpu.VMEM((2,) + block, f32),
            dma((3,)),
            dma((3, N_GROUP)),
            dma((3, N_GROUP)),
            dma((2, 2, 5, 2)),
            dma((2, 2, 5, 2)),
            dma((2,)),
            dma((2,)),
            dma((2, 2, NZ, 2)),
            dma((2, 2, NZ, 2)),
            dma((2, 2, NZ, 2)),
            dma((2, 2, NZ, 2)),
            dma((2, 2, 5, 2)),
            dma((2, 2, 5, 2)),
            dma((2,)),
            dma((2,)),
            dma((2, NZ, 2)),
            dma((2, NZ, 2)),
        ],
        compiler_params=pltpu.CompilerParams(
            collective_id=0, has_side_effects=True, vmem_limit_bytes=62 << 20
        ),
        name="inner_step",
    )(clip, target, time_proj, embed, w1, w2, r1, r2)


def embed_rows(step_index, ident, subject_table):
    half_width = subject_table.shape[1] // 2
    freqs = jnp.exp(-math.log(10000.0) * jnp.arange(half_width, dtype=jnp.float32) / half_width)
    angles = step_index.astype(jnp.float32) * freqs
    embedding = jnp.concatenate([jnp.cos(angles), jnp.sin(angles)])
    onehot = (jnp.arange(subject_table.shape[0], dtype=jnp.int32) == ident).astype(jnp.float32)
    embedding = embedding + jnp.dot(onehot, subject_table, precision=lax.Precision.HIGHEST)
    activated = jax.nn.silu(embedding).astype(jnp.bfloat16)
    return jnp.broadcast_to(activated[None, :], (16, activated.shape[0]))


def shards(
    clips,
    targets,
    timestep,
    identity,
    conv1_weight,
    conv2_weight,
    rate1,
    rate2,
    time_proj,
    subject_table,
):
    embed = embed_rows(timestep[0], identity[0], subject_table)
    adapted_one, adapted_two = step(
        clips.reshape(POINTS, C),
        targets.reshape(POINTS, C),
        time_proj,
        embed,
        conv1_weight,
        conv2_weight,
        rate1,
        rate2,
    )
    return (adapted_one[None], adapted_two[None])


def solution(mesh):
    return jax.shard_map(
        shards,
        mesh=mesh,
        in_specs=(
            P(("group", "member"), None, None, None),
            P(("group", "member"), None, None, None),
            P(("group", "member")),
            P(("group", "member")),
            P("member", "group"),
            P("member", "group"),
            P("member", "group"),
            P("member", "group"),
            P(),
            P(),
        ),
        out_specs=(P("group", "member", None), P("group", "member", None)),
        check_vma=False,
    )
```

```python
import functools
import math

import jax
import jax.numpy as jnp
from jax import lax
from jax.experimental import pallas as pl
from jax.experimental.pallas import tpu as pltpu
from jax.sharding import PartitionSpec as P

GN_GROUPS = 32
MESH = pl.DeviceIdType.MESH
N_GROUP, N_MEMBER, NZ, NC, NX = 8, 32, 8, 2, 2
ROWS, COLS, C = 60, 80, 640
TAPS = 3 * C
FRAMES, HW = 14, 64
POINTS = FRAMES * HW
PER_GROUP = C // GN_GROUPS
SCALE = 1.0 / math.sqrt(TAPS)
UNIT = 128
PART = 32


class Place:
    def __init__(self):
        self.g = lax.axis_index("group")
        self.m = lax.axis_index("member")
        self.core = lax.rem(self.m, 2)
        self.q = lax.div(self.m, 2)
        self.z = lax.rem(self.q, NZ)
        self.xh = lax.div(self.q, NZ)
        self.up = self.at(self.xh, self.zof(1), self.core)
        self.down = self.at(self.xh, self.zof(-1), self.core)
        self.across = self.at(1 - self.xh, self.z, self.core)
        self.sibling = self.at(self.xh, self.z, 1 - self.core)
        self.x_lo = lax.rem(self.g, 2)
        self.y_lo = lax.rem(lax.div(self.g, 2), 2)
        self.beside_x = (self.g + 1 - 2 * self.x_lo, self.m)
        self.beside_y = (self.g + 2 - 4 * self.y_lo, self.m)

    def at(self, xh, z, core):
        return (self.g, (xh * NZ + z) * 2 + core)

    def zof(self, step):
        return lax.rem(self.z + (step + NZ), NZ)

    def peer(self, step):
        return lax.rem(self.g + step, N_GROUP)

    def xof(self, piece):
        return self.xh if piece == 0 else 1 - self.xh


def remote(src, dst, send, recv, device):
    return pltpu.make_async_remote_copy(
        src_ref=src, dst_ref=dst, send_sem=send, recv_sem=recv, device_id=device, device_id_type=MESH
    )


def enter(place, with_group):
    barrier = pltpu.get_barrier_semaphore()
    partners = [place.up, place.down, place.across, place.sibling]
    if with_group:
        partners += [(place.peer(step), place.m) for step in range(1, N_GROUP)]
    for partner in partners:
        pl.semaphore_signal(barrier, inc=1, device_id=partner, device_id_type=MESH)
    pl.semaphore_wait(barrier, len(partners))


def exists(direction, dist, piece):
    return dist < 4 or (dist == 4 and piece == direction)


def step_kernel(
    clip_hbm, target_hbm, proj_hbm, embed, w1, w2, r1, r2, total_out, own,
    clip, target, proj, same_group, act_one, act_two, err, grad_hid, flip_one, flip_two, hid, weights, grad,
    gbuf, wbuf, blocks, sib_in, cross_out, cross_in, hop_out, hop_in, last_out, last_in, x_out, x_out_own, x_in,
    load_sem, gsend, grecv, zsend, zrecv, xsend, xrecv, ssend, srecv, bsend, brecv,
    rsend, rrecv, ysend, yrecv, psend, precv, csend, crecv,
):
    f32, bf16 = jnp.float32, jnp.bfloat16
    place = Place()
    sends = []

    def go(copy):
        copy.start()
        sends.append(copy)

    loads = [
        pltpu.make_async_copy(src, dst, load_sem.at[i])
        for i, (src, dst) in enumerate(((clip_hbm, clip), (proj_hbm, proj), (target_hbm, target)))
    ]
    for load in loads:
        load.start()
    for index, ref in enumerate((w1, w2, r1, r2)):
        gbuf[index, place.g] = ref[...]
    enter(place, True)

    def group_copy(part, step, here):
        block = pl.ds(part, 1) if part < 2 else pl.ds(2, 2)
        source = place.g if here else lax.rem(place.g + (N_GROUP - step), N_GROUP)
        ref = gbuf.at[block, source]
        return remote(ref, ref, gsend.at[part, step], grecv.at[part, step], (place.peer(step), place.m))

    def group_send(part):
        for step in range(1, N_GROUP):
            go(group_copy(part, step, True))

    group_send(0)
    group_send(1)

    def assemble(index):
        parts = [gbuf[index, group].astype(f32) for group in range(N_GROUP)]
        return jnp.concatenate(parts, axis=1)

    tile_slot = (2 * place.x_lo, 2 - 2 * place.x_lo, 1 + 2 * place.y_lo, 3 - 2 * place.y_lo)

    def slot(w, dist, piece, first, count, core=None):
        core = place.core if core is None else core
        return wbuf.at[w, place.xof(piece), place.zof(-dist), core, pl.ds(first, count)]

    def share_copy(w, dist, piece, high, count, here):
        ref = slot(w, dist, piece, 2 * high, count, place.core if here else 1 - place.core)
        at = (w, high, dist % NZ, piece)
        return remote(ref, ref, ssend.at[at], srecv.at[at], place.sibling)

    def side_copy(w, side, dist, piece):
        src, dst = slot(w, dist, piece, side, 1), slot(w, dist, piece, side + 2, 1)
        at = (w, side, dist % NZ, piece)
        return remote(src, dst, bsend.at[at], brecv.at[at], (place.beside_x, place.beside_y)[side])

    def ring_copy(w, direction, dist, piece, here):
        sign = 1 if direction == 0 else -1
        ref = slot(w, sign * (dist - 1 if here else dist), piece, 0, 2)
        to = place.up if direction == 0 else place.down
        return remote(ref, ref, zsend.at[w, direction, dist, piece], zrecv.at[w, direction, dist, piece], to)

    def forward(w, direction, dist, piece):
        if exists(direction, dist, piece):
            go(ring_copy(w, direction, dist, piece, True))

    def hand_on(w, dist, piece):
        for side in range(2):
            go(side_copy(w, side, dist, piece))
        go(share_copy(w, dist, piece, 0, 2, True))

    def across_copy(w, piece):
        ref = slot(w, 0, piece, 0, 2)
        return remote(ref, ref, xsend.at[w], xrecv.at[w], place.across)

    def ring_start(w):
        for step in range(1, N_GROUP):
            group_copy(w, step, False).wait_recv()
        whole = jnp.concatenate([assemble(w), jnp.zeros((4, C), f32)], axis=0).astype(bf16)
        own[w] = whole[0:ROWS]
        for tile in range(4):
            wbuf[w, place.xh, place.z, place.core, tile_slot[tile]] = whole[16 * tile : 16 * (tile + 1)]
        go(across_copy(w, 0))
        for direction in range(2):
            forward(w, direction, 1, 0)
        go(share_copy(w, 0, 0, 0, 4, True))

    def ring_across(w):
        across_copy(w, 1).wait_recv()
        for direction in range(2):
            forward(w, direction, 1, 1)
        hand_on(w, 0, 1)

    def ring_step(w, dist):
        for piece in range(2):
            for direction in range(2):
                if exists(direction, dist, piece):
                    ring_copy(w, direction, dist, piece, False).wait_recv()
                    forward(w, direction, dist + 1, piece)
            for direction in range(2):
                if exists(direction, dist, piece):
                    hand_on(w, dist if direction == 0 else -dist, piece)

    def ring_sides(w, dist):
        for piece in range(2):
            for direction in range(2):
                far = dist if direction == 0 else -dist
                if not exists(direction, dist, piece) or dist == 0 and (direction == 1 or piece == 0):
                    continue
                for side in range(2):
                    side_copy(w, side, far, piece).wait_recv()
                go(share_copy(w, far, piece, 1, 2, True))

    def dense(w):
        for dist in range(NZ):
            for piece in range(2):
                if (dist, piece) == (0, 0):
                    share_copy(w, dist, piece, 0, 4, False).wait_recv()
                else:
                    share_copy(w, dist, piece, 0, 2, False).wait_recv()
                    share_copy(w, dist, piece, 1, 2, False).wait_recv()
        for m in range(N_MEMBER):
            for tile in range(4):
                start, size = ROWS * m + 16 * tile, min(16, ROWS - 16 * tile)
                block = wbuf[w, m // 16, (m // 2) % NZ, m % 2, tile_slot[tile]]
                weights[w, start : start + size, :] = block[0:size]

    def lay(w):
        for m in range(N_MEMBER):
            for part in range(2):
                start = ROWS * m + PART * part
                blocks[w, m // 16, (m // 2) % NZ, m % 2, part] = grad[start : start + PART, :]

    def pair_copy(w, dist, piece):
        src = blocks.at[w, place.xof(piece), place.zof(dist), 1 - place.core]
        dst = sib_in.at[w, dist, piece]
        return remote(src, dst, psend.at[w, dist, piece], precv.at[w, dist, piece], place.sibling)

    def pair(w):
        for dist in (4, 3, 5, 2, 6, 1, 7, 0):
            for piece in (1, 0):
                go(pair_copy(w, dist, piece))

    paired = set()

    def summed(w, dist, piece, part):
        if (w, dist, piece) not in paired:
            paired.add((w, dist, piece))
            pair_copy(w, dist, piece).wait_recv()
        return blocks[w, place.xof(piece), place.zof(dist), place.core, part] + sib_in[w, dist, piece, part]

    def cross_copy(w, dist):
        return remote(cross_out.at[w, dist], cross_in.at[w, dist], csend.at[w, dist], crecv.at[w, dist], place.across)

    def cross(w, *dists):
        for dist in dists:
            cross_out[w, dist] = summed(w, dist, 1, 0).astype(bf16)
            go(cross_copy(w, dist))

    def crossed(w, dist):
        cross_copy(w, dist).wait_recv()
        return summed(w, dist, 0, 0) + cross_in[w, dist].astype(f32)

    def hop(w, part, direction, dist):
        to = place.up if direction == 0 else place.down
        if dist == 1:
            src, dst = last_out.at[w, direction], last_in.at[w, direction]
        else:
            src, dst = hop_out.at[w, direction, dist - 2], hop_in.at[w, direction, dist - 2]
        if part == 1:
            take = pl.ds(direction, 1) if dist == 4 else pl.ds(0, 2)
            src, dst = src.at[take], dst.at[take]
        else:
            take = pl.ds(16 * direction, 16) if dist == 4 else pl.ds(0, PART)
            src, dst = src.at[2, take], dst.at[2, take]
        return src, dst, remote(src, dst, rsend.at[w, part, direction, dist], rrecv.at[w, part, direction, dist], to)

    def far(direction, dist):
        return dist if direction == 0 else NZ - dist

    def ring_z(w, dist):
        for direction in range(2):
            arrived = None
            if dist < 4:
                _, arrived, copy = hop(w, 1, direction, dist + 1)
                copy.wait_recv()
            src, _, copy = hop(w, 1, direction, dist)
            for piece in (direction,) if dist == 4 else (0, 1):
                total = summed(w, far(direction, dist), piece, 1)
                if dist < 3:
                    total = total + arrived[piece].astype(f32)
                elif dist == 3 and piece == direction:
                    total = total + arrived[0].astype(f32)
                src[0 if dist == 4 else piece] = total.astype(src.dtype)
            go(copy)

    def ring_x(w, dist):
        own_sum = crossed(w, 4) if dist == 4 else None
        for direction in range(2):
            src, _, copy = hop(w, 0, direction, dist)
            if dist == 4:
                src[...] = own_sum[16 * direction : 16 * (direction + 1)].astype(src.dtype)
            else:
                _, arrived, before = hop(w, 0, direction, dist + 1)
                total = crossed(w, far(direction, dist))
                before.wait_recv()
                if dist == 3:
                    low, high = total[:16], total[16:]
                    if direction == 0:
                        low = low + arrived[...].astype(f32)
                    else:
                        high = high + arrived[...].astype(f32)
                    src[0:16] = low.astype(src.dtype)
                    src[16:PART] = high.astype(src.dtype)
                else:
                    src[...] = (total + arrived[...].astype(f32)).astype(src.dtype)
            go(copy)

    def swap_copy(w):
        return remote(x_out.at[w], x_in.at[w], ysend.at[w], yrecv.at[w], place.across)

    def finish_z(w):
        parts = [summed(w, 0, piece, 1) for piece in range(2)]
        for direction in range(2):
            _, arrived, copy = hop(w, 1, direction, 1)
            copy.wait_recv()
            parts = [parts[piece] + arrived[piece] for piece in range(2)]
        x_out[w] = parts[1]
        go(swap_copy(w))
        x_out_own[w] = parts[0]

    def finish_x(w):
        total = crossed(w, 0)
        for direction in range(2):
            _, arrived, copy = hop(w, 0, direction, 1)
            copy.wait_recv()
            total = total + arrived[...]
        total_out[w, 0:PART] = SCALE * total

    def finish(w):
        swap_copy(w).wait_recv()
        total_out[w, PART:ROWS] = (SCALE * (x_out_own[w] + x_in[w]))[0 : ROWS - PART]

    def scatter(w):
        cross(w, 4)
        ring_z(w, 4)
        yield
        cross(w, 3, 5)
        yield
        ring_z(w, 3)
        cross(w, 2, 6)
        yield
        ring_x(w, 4)
        yield
        ring_z(w, 2)
        cross(w, 1, 7, 0)
        yield
        ring_x(w, 3)
        yield
        ring_z(w, 1)
        yield
        ring_x(w, 2)
        yield
        finish_z(w)
        yield
        ring_x(w, 1)
        yield
        finish_x(w)
        yield
        finish(w)

    def rows(index, size=UNIT):
        return pl.ds(index * size, size)

    def fold(values):
        return values.reshape(values.shape[0] // 8, 8, C).sum(axis=0)

    def spread(sums):
        column = sums.sum(axis=0, keepdims=True)
        top = column.astype(bf16)
        rest = column - top.astype(f32)
        middle = rest.astype(bf16)
        low = (rest - middle.astype(f32)).astype(bf16)
        terms = jnp.concatenate([top, middle, low, jnp.zeros((13, C), bf16)], axis=0)
        total = jnp.dot(terms, same_group[...], preferred_element_type=f32)
        return total.sum(axis=0, keepdims=True) * (1.0 / (POINTS * PER_GROUP))

    def sweep(body, start):
        return lax.fori_loop(0, FRAMES, lambda i, carry: body(pl.ds(pl.multiple_of(i * HW, HW), HW), carry), start)

    def padded(i):
        return pl.ds(HW + i * UNIT, UNIT)

    def silu(v):
        return v / (1.0 + jnp.exp(-v))

    first = lax.broadcasted_iota(jnp.int32, (C, C), 0)
    second = lax.broadcasted_iota(jnp.int32, (C, C), 1)
    same_group[...] = (((first * 3277) >> 16) == ((second * 3277) >> 16)).astype(f32).astype(bf16)
    blank = jnp.zeros((HW, C), bf16)
    for ref in (act_one, act_two, err, grad_hid):
        ref[0:HW, :] = blank
        ref[HW + POINTS :, :] = blank
    zero = jnp.zeros((8, C), f32)
    grad[TAPS:, :] = zero
    loads[0].wait()
    centre = spread(sweep(lambda at, acc: acc + fold(clip[at, :].astype(f32)), zero))

    def squares(ref, mean):
        def body(at, acc):
            off = ref[at, :].astype(f32) - mean
            return acc + fold(off * off)

        return lax.rsqrt(spread(sweep(body, zero)) + 1e-05)

    inverse = squares(clip, centre)
    units = POINTS // UNIT

    def act_unit(i):
        values = (clip[rows(i), :].astype(f32) - centre) * inverse
        act_one[padded(i), :] = silu(values).astype(bf16)

    def flip_unit(flipped, ref, i):
        flipped[:, rows(i)] = ref[padded(i), :].T

    ring_start(0)
    act_unit(0)
    act_unit(1)
    act_unit(2)
    ring_across(0)
    ring_start(1)
    act_unit(3)
    ring_step(0, 1)
    act_unit(4)
    ring_across(1)
    ring_sides(0, 0)
    act_unit(5)
    ring_step(0, 2)
    ring_step(1, 1)
    act_unit(6)
    ring_sides(0, 1)
    loads[1].wait()
    bias = jnp.dot(embed[...], proj[...], preferred_element_type=f32)[0:1]
    ring_step(0, 3)
    ring_step(1, 2)
    ring_sides(1, 0)
    for i in range(3):
        flip_unit(flip_one, act_one, i)
    ring_sides(0, 2)
    ring_step(0, 4)
    ring_step(1, 3)
    ring_sides(1, 1)
    for i in range(3, units):
        flip_unit(flip_one, act_one, i)
    ring_sides(0, 3)
    ring_sides(0, 4)
    ring_step(1, 4)
    ring_sides(1, 2)
    dense(0)

    def stacked(ref, start, size, taps):
        return jnp.concatenate([ref[pl.ds(start + HW * tap, size), :] for tap in taps], axis=1)

    half = POINTS // 2
    sums = zero
    for part in range(2):
        mixed = jnp.dot(stacked(act_one, part * half, half, (0, 1, 2)), weights[0], preferred_element_type=f32)
        values = SCALE * mixed + bias
        hid[pl.ds(part * half, half), :] = values
        sums = sums + fold(values)
        ring_sides(1, 3 + part)
    group_send(2)
    centre_two = spread(sums)
    inverse_two = squares(hid, centre_two)
    for i in range(units):
        values = (hid[rows(i), :] - centre_two) * inverse_two
        hid[rows(i), :] = values
        act_two[padded(i), :] = silu(values).astype(bf16)
    for i in range(units):
        flip_unit(flip_two, act_two, i)
    dense(1)
    loads[2].wait()

    for part in range(2):
        at = pl.ds(part * half, half)
        mixed = jnp.dot(stacked(act_two, part * half, half, (0, 1, 2)), weights[1], preferred_element_type=f32)
        output = clip[at, :].astype(f32) + SCALE * mixed
        err[pl.ds(HW + part * half, half), :] = (output - target[at, :].astype(f32)).astype(bf16)

    def weight_grad(flipped, ref, tap):
        grad[C * tap : C * (tap + 1), :] = jnp.dot(
            flipped[...], ref[pl.ds(HW * (2 - tap), POINTS), :], preferred_element_type=f32
        )

    for tap in range(3):
        weight_grad(flip_two, err, tap)
    lay(1)
    pair(1)

    scatter_two = scatter(1)
    sum_grad, sum_mixed = zero, zero
    for part in range(2):
        at = pl.ds(part * half, half)
        back = jnp.zeros((half, C), f32)
        for tap in range(3):
            back = back + lax.dot_general(
                err[pl.ds(part * half + HW * (2 - tap), half), :],
                weights[1, C * tap : C * (tap + 1), :],
                (((1,), (1,)), ((), ())),
                preferred_element_type=f32,
            )
        values = hid[at, :]
        gate = 1.0 / (1.0 + jnp.exp(-values))
        inner = (SCALE * back) * (gate * (1.0 + values * (1.0 - gate)))
        grad[at, :] = inner
        sum_grad = sum_grad + fold(inner)
        sum_mixed = sum_mixed + fold(inner * values)
        next(scatter_two)
        next(scatter_two)
    mean_grad, mean_mixed = spread(sum_grad), spread(sum_mixed)
    for i in range(units):
        inner = grad[rows(i), :] - mean_grad - hid[rows(i), :] * mean_mixed
        grad_hid[padded(i), :] = (inner * inverse_two).astype(bf16)
    for tap in range(3):
        weight_grad(flip_one, grad_hid, tap)
        next(scatter_two)
    lay(0)
    pair(0)
    for step in range(1, N_GROUP):
        group_copy(2, step, False).wait_recv()
    own[2] = assemble(2).astype(bf16)
    own[3] = assemble(3).astype(bf16)
    scatter_one = scatter(0)
    next(scatter_one)
    for _ in scatter_two:
        next(scatter_one, None)
    for _ in scatter_one:
        pass
    for copy in sends:
        copy.wait_send()


def step(clip, target, time_proj, embed, w1, w2, r1, r2):
    f32, bf16 = jnp.float32, jnp.bfloat16
    dma = pltpu.SemaphoreType.DMA
    vmem = pl.BlockSpec(memory_space=pltpu.VMEM)
    anywhere = pl.BlockSpec(memory_space=pl.ANY)
    part = (PART, C)
    wide = (POINTS + 2 * HW, C)
    return pl.pallas_call(
        step_kernel,
        out_shape=(jax.ShapeDtypeStruct((2, ROWS, C), f32), jax.ShapeDtypeStruct((4, ROWS, C), bf16)),
        in_specs=[anywhere] * 3 + [vmem] * 5,
        out_specs=(vmem,) * 2,
        scratch_shapes=[
            pltpu.VMEM((POINTS, C), bf16),
            pltpu.VMEM((POINTS, C), bf16),
            pltpu.VMEM(time_proj.shape, bf16),
            pltpu.VMEM((C, C), bf16),
            pltpu.VMEM(wide, bf16),
            pltpu.VMEM(wide, bf16),
            pltpu.VMEM(wide, bf16),
            pltpu.VMEM(wide, bf16),
            pltpu.VMEM((C, POINTS), bf16),
            pltpu.VMEM((C, POINTS), bf16),
            pltpu.VMEM((POINTS, C), f32),
            pltpu.VMEM((2, TAPS, C), bf16),
            pltpu.VMEM((TAPS + 8, C), f32),
            pltpu.VMEM((4, N_GROUP, ROWS, COLS), bf16),
            pltpu.VMEM((2, NX, NZ, NC, 4, 16, C), bf16),
            pltpu.VMEM((2, NX, NZ, NC, 2) + part, f32),
            pltpu.VMEM((2, NZ, 2, 2) + part, f32),
            pltpu.VMEM((2, NZ) + part, bf16),
            pltpu.VMEM((2, NZ) + part, bf16),
            pltpu.VMEM((2, 2, 3, 3) + part, bf16),
            pltpu.VMEM((2, 2, 3, 3) + part, bf16),
            pltpu.VMEM((2, 2, 3) + part, f32),
            pltpu.VMEM((2, 2, 3) + part, f32),
            pltpu.VMEM((2,) + part, f32),
            pltpu.VMEM((2,) + part, f32),
            pltpu.VMEM((2,) + part, f32),
            dma((3,)),
            dma((3, N_GROUP)),
            dma((3, N_GROUP)),
            dma((2, 2, 5, 2)),
            dma((2, 2, 5, 2)),
            dma((2,)),
            dma((2,)),
            dma((2, 2, NZ, 2)),
            dma((2, 2, NZ, 2)),
            dma((2, 2, NZ, 2)),
            dma((2, 2, NZ, 2)),
            dma((2, 2, 2, 5)),
            dma((2, 2, 2, 5)),
            dma((2,)),
            dma((2,)),
            dma((2, NZ, 2)),
            dma((2, NZ, 2)),
            dma((2, NZ)),
            dma((2, NZ)),
        ],
        compiler_params=pltpu.CompilerParams(
            collective_id=0, has_side_effects=True, vmem_limit_bytes=62 << 20
        ),
        name="inner_step",
    )(clip, target, time_proj, embed, w1, w2, r1, r2)


def embed_rows(step_index, ident, subject_table):
    half_width = subject_table.shape[1] // 2
    freqs = jnp.exp(-math.log(10000.0) * jnp.arange(half_width, dtype=jnp.float32) / half_width)
    angles = step_index.astype(jnp.float32) * freqs
    embedding = jnp.concatenate([jnp.cos(angles), jnp.sin(angles)])
    onehot = (jnp.arange(subject_table.shape[0], dtype=jnp.int32) == ident).astype(jnp.float32)
    embedding = embedding + jnp.dot(onehot, subject_table, precision=lax.Precision.HIGHEST)
    activated = jax.nn.silu(embedding).astype(jnp.bfloat16)
    return jnp.broadcast_to(activated[None, :], (16, activated.shape[0]))


def shards(
    clips,
    targets,
    timestep,
    identity,
    conv1_weight,
    conv2_weight,
    rate1,
    rate2,
    time_proj,
    subject_table,
):
    embed = embed_rows(timestep[0], identity[0], subject_table)
    total, own = step(
        clips.reshape(POINTS, C),
        targets.reshape(POINTS, C),
        time_proj,
        embed,
        conv1_weight,
        conv2_weight,
        rate1,
        rate2,
    )
    own = own.astype(jnp.float32)
    return tuple((own[w] - own[2 + w] * total[w])[None] for w in range(2))


def solution(mesh):
    return jax.shard_map(
        shards,
        mesh=mesh,
        in_specs=(
            P(("group", "member"), None, None, None),
            P(("group", "member"), None, None, None),
            P(("group", "member")),
            P(("group", "member")),
            P("member", "group"),
            P("member", "group"),
            P("member", "group"),
            P("member", "group"),
            P(),
            P(),
        ),
        out_specs=(P("group", "member", None), P("group", "member", None)),
        check_vma=False,
    )
```

```python
import functools
import math

import jax
import jax.numpy as jnp
import numpy as np
from jax import lax
from jax.experimental import pallas as pl
from jax.experimental.pallas import tpu as pltpu
from jax.sharding import PartitionSpec as P

GN_GROUPS = 32
MESH = pl.DeviceIdType.MESH
N_GROUP, N_MEMBER, NZ, NC, NX = 8, 32, 8, 2, 2
ROWS, COLS, C = 60, 80, 640
TAPS = 3 * C
FRAMES, HW = 14, 64
POINTS = FRAMES * HW
PER_GROUP = C // GN_GROUPS
SCALE = 1.0 / math.sqrt(TAPS)
UNIT = 128
PART = 32


class Place:
    def __init__(self):
        self.g = lax.axis_index("group")
        self.m = lax.axis_index("member")
        self.core = lax.rem(self.m, 2)
        self.q = lax.div(self.m, 2)
        self.z = lax.rem(self.q, NZ)
        self.xh = lax.div(self.q, NZ)
        self.up = self.at(self.xh, self.zof(1), self.core)
        self.down = self.at(self.xh, self.zof(-1), self.core)
        self.across = self.at(1 - self.xh, self.z, self.core)
        self.sibling = self.at(self.xh, self.z, 1 - self.core)
        self.x_lo = lax.rem(self.g, 2)
        self.y_lo = lax.rem(lax.div(self.g, 2), 2)
        self.beside_x = (self.g + 1 - 2 * self.x_lo, self.m)
        self.beside_y = (self.g + 2 - 4 * self.y_lo, self.m)
        self.opposite = self.across[1]
        self.twin = self.sibling[1]

    def at(self, xh, z, core):
        return (self.g, (xh * NZ + z) * 2 + core)

    def zof(self, step):
        return lax.rem(self.z + (step + NZ), NZ)

    def peer(self, step):
        return lax.rem(self.g + step, N_GROUP)

    def xof(self, piece):
        return self.xh if piece == 0 else 1 - self.xh


def remote(src, dst, send, recv, device):
    return pltpu.make_async_remote_copy(
        src_ref=src, dst_ref=dst, send_sem=send, recv_sem=recv, device_id=device, device_id_type=MESH
    )


def partners(place):
    plane = [((place.peer(step), place.m)) for step in range(1, N_GROUP)]
    beyond = [((place.peer(step), place.opposite)) for step in range(N_GROUP)]
    sides = [(place.beside_x[0], place.twin), (place.beside_y[0], place.twin)]
    return plane + beyond + sides + [place.up, place.down, place.sibling]


def exists(direction, dist, piece):
    return dist < 4 or (dist == 4 and piece == direction)


def step_kernel(
    t_ref, ident_ref, freqs, table, clip_hbm, target_hbm, proj_hbm, w1, w2, r1, r2, update, kept,
    clip, target, proj, same_group, act_one, act_two, err, grad_hid, flip_one, flip_two, hid, weights, grad,
    gbuf, rbuf, wbuf, blocks, sib_in, cross_out, cross_in, hop_out, hop_in, last_out, last_in, x_out, x_in, rate_rows,
    load_sem, gsend, grecv, rate_send, rate_recv, zsend, zrecv, ssend, srecv, bsend, brecv, tsend, trecv,
    rsend, rrecv, ysend, yrecv, psend, precv, csend, crecv,
):
    f32, bf16 = jnp.float32, jnp.bfloat16
    place = Place()
    sends = []

    def go(copy):
        copy.start()
        sends.append(copy)

    barrier = pltpu.get_barrier_semaphore()
    friends = partners(place)
    for friend in friends:
        pl.semaphore_signal(barrier, inc=1, device_id=friend, device_id_type=MESH)
    for index, ref in enumerate((w1, w2)):
        gbuf[index, 0, place.g] = ref[...]
    for index, ref in enumerate((r1, r2)):
        rbuf[index, place.g] = ref[...]
    first = lax.broadcasted_iota(jnp.int32, (C, C), 0)
    second = lax.broadcasted_iota(jnp.int32, (C, C), 1)
    same_group[...] = (((first * 3277) >> 16) == ((second * 3277) >> 16)).astype(f32).astype(bf16)
    blank = jnp.zeros((HW, C), bf16)
    for ref in (act_one, act_two, err, grad_hid):
        ref[0:HW, :] = blank
        ref[HW + POINTS :, :] = blank
    zero = jnp.zeros((8, C), f32)
    grad[TAPS:, :] = zero
    pl.semaphore_wait(barrier, len(friends))

    def group_copy(w, beyond, step, here):
        source = place.g if here else lax.rem(place.g + (N_GROUP - step), N_GROUP)
        to = (place.peer(step), place.opposite if beyond else place.m)
        at = (w, beyond, step)
        return remote(gbuf.at[w, 0, source if not beyond else place.g], gbuf.at[w, beyond, source],
                      gsend.at[at], grecv.at[at], to)

    def group_send(w):
        for beyond in range(2):
            for step in range(1 - beyond, N_GROUP):
                go(group_copy(w, beyond, step, True))

    def rate_copy(step, here):
        source = place.g if here else lax.rem(place.g + (N_GROUP - step), N_GROUP)
        ref = rbuf.at[:, source]
        return remote(ref, ref, rate_send.at[step], rate_recv.at[step], (place.peer(step), place.m))

    group_send(0)
    loads = [
        pltpu.make_async_copy(src, dst, load_sem.at[i])
        for i, (src, dst) in enumerate(((clip_hbm, clip), (proj_hbm, proj), (target_hbm, target)))
    ]
    loads[0].start()
    loads[1].start()

    def assemble(read):
        return jnp.concatenate([read(group).astype(f32) for group in range(N_GROUP)], axis=1)

    tile_slot = (2 * place.x_lo, 2 - 2 * place.x_lo, 1 + 2 * place.y_lo, 3 - 2 * place.y_lo)

    def slot(w, dist, piece, first, count):
        return wbuf.at[w, place.zof(-dist), place.core, place.xof(piece), pl.ds(first, count)]

    def slots(w, dist, first, count, core=None):
        core = place.core if core is None else core
        return wbuf.at[w, place.zof(-dist), core, :, pl.ds(first, count)]

    def share_copy(w, dist, high, count, here):
        ref = slots(w, dist, 2 * high, count, place.core if here else 1 - place.core)
        at = (w, high, dist % NZ)
        return remote(ref, ref, ssend.at[at], srecv.at[at], place.sibling)

    def side_copy(w, side, dist):
        src, dst = slots(w, dist, side, 1), slots(w, dist, side + 2, 1)
        at = (w, side, dist % NZ)
        return remote(src, dst, bsend.at[at], brecv.at[at], (place.beside_x, place.beside_y)[side])

    def ring_copy(w, direction, dist, piece, here):
        sign = 1 if direction == 0 else -1
        ref = slot(w, sign * (dist - 1 if here else dist), piece, 0, 2)
        to = place.up if direction == 0 else place.down
        return remote(ref, ref, zsend.at[w, direction, dist, piece], zrecv.at[w, direction, dist, piece], to)

    def forward(w, direction, dist, piece):
        if exists(direction, dist, piece):
            go(ring_copy(w, direction, dist, piece, True))

    def end_copy(w, side):
        src, dst = slots(w, 4, side, 1), slots(w, 4, side + 2, 1)
        to = ((place.beside_x, place.beside_y)[side][0], place.twin)
        return remote(src, dst, tsend.at[w, side], trecv.at[w, side], to)

    def end_in(w, side):
        ref = slots(w, 4, side + 2, 1, 1 - place.core)
        return remote(ref, ref, tsend.at[w, side], trecv.at[w, side], place.sibling)

    def hand_on(w, dist):
        for side in range(2):
            go(side_copy(w, side, dist))
            if dist == 4:
                go(end_copy(w, side))
        go(share_copy(w, dist, 0, 2, True))

    def plane_block(w, piece):
        for step in range(1 - piece, N_GROUP):
            group_copy(w, piece, step, False).wait_recv()
        rows_f32 = assemble(lambda group: gbuf[w, piece, group])
        whole = jnp.concatenate([rows_f32, jnp.zeros((4, C), f32)], axis=0).astype(bf16)
        if piece == 0:
            kept[w] = rows_f32
        for tile in range(4):
            wbuf[w, place.z, place.core, place.xof(piece), tile_slot[tile]] = whole[16 * tile : 16 * (tile + 1)]
        for direction in range(2):
            forward(w, direction, 1, piece)

    def ring_start(w):
        for piece in range(2):
            plane_block(w, piece)
        go(share_copy(w, 0, 0, 4, True))

    def ring_step(w, dist):
        for piece in range(2):
            for direction in range(2):
                if exists(direction, dist, piece):
                    ring_copy(w, direction, dist, piece, False).wait_recv()
                    forward(w, direction, dist + 1, piece)
        for far in sorted({dist, NZ - dist}):
            hand_on(w, far)

    def ring_sides(w, dist):
        for far in sorted({dist, NZ - dist}):
            for side in range(2):
                side_copy(w, side, far).wait_recv()
            if dist < 4:
                go(share_copy(w, far, 1, 2, True))

    def dense(w):
        for dist in range(NZ):
            share_copy(w, dist, 0, 2 if dist else 4, False).wait_recv()
            if dist == 4:
                for side in range(2):
                    end_in(w, side).wait_recv()
            elif dist:
                share_copy(w, dist, 1, 2, False).wait_recv()
        for m in range(N_MEMBER):
            for tile in range(4):
                start, size = ROWS * m + 16 * tile, min(16, ROWS - 16 * tile)
                block = wbuf[w, (m // 2) % NZ, m % 2, m // 16, tile_slot[tile]]
                weights[w, start : start + size, :] = block[0:size]

    def lay(w):
        for m in range(N_MEMBER):
            for part in range(2):
                start = ROWS * m + PART * part
                blocks[w, m // 16, (m // 2) % NZ, m % 2, part] = grad[start : start + PART, :]

    def pair_copy(w, dist, piece):
        src = blocks.at[w, place.xof(piece), place.zof(dist), 1 - place.core]
        dst = sib_in.at[w, dist, piece]
        return remote(src, dst, psend.at[w, dist, piece], precv.at[w, dist, piece], place.sibling)

    def pair(w):
        for dist in (4, 3, 5, 2, 6, 1, 7, 0):
            for piece in (1, 0):
                go(pair_copy(w, dist, piece))

    paired = set()

    def summed(w, dist, piece, part):
        if (w, dist, piece) not in paired:
            paired.add((w, dist, piece))
            pair_copy(w, dist, piece).wait_recv()
        return blocks[w, place.xof(piece), place.zof(dist), place.core, part] + sib_in[w, dist, piece, part]

    def cross_copy(w, dist):
        at = (w, dist)
        return remote(cross_out.at[at], cross_in.at[at], csend.at[at], crecv.at[at], place.across)

    def cross(w, *dists):
        for dist in dists:
            cross_out[w, dist] = summed(w, dist, 1, 0).astype(bf16)
            go(cross_copy(w, dist))

    def crossed(w, dist):
        cross_copy(w, dist).wait_recv()
        return summed(w, dist, 0, 0) + cross_in[w, dist].astype(f32)

    def hop(w, lane, direction, dist):
        at = (w, lane, direction, dist)
        to = place.up if direction == 0 else place.down
        if dist == 1:
            src, dst = last_out.at[w, direction, lane], last_in.at[w, direction, lane]
        else:
            src, dst = hop_out.at[w, direction, dist - 2, lane], hop_in.at[w, direction, dist - 2, lane]
        if lane == 2 and dist == 4:
            src, dst = src.at[pl.ds(16 * direction, 16)], dst.at[pl.ds(16 * direction, 16)]
        return src, dst, remote(src, dst, rsend.at[at], rrecv.at[at], to)

    def far(direction, dist):
        return dist if direction == 0 else NZ - dist

    def ring_z(w, dist):
        for piece in (1, 0):
            for direction in range(2):
                if not exists(direction, dist, piece):
                    continue
                total = summed(w, far(direction, dist), piece, 1)
                if exists(direction, dist + 1, piece):
                    _, arrived, copy = hop(w, piece, direction, dist + 1)
                    copy.wait_recv()
                    total = total + arrived[...].astype(f32)
                src, _, copy = hop(w, piece, direction, dist)
                src[...] = total.astype(src.dtype)
                go(copy)

    def ring_x(w, dist):
        own_sum = crossed(w, 4) if dist == 4 else None
        for direction in range(2):
            src, _, copy = hop(w, 2, direction, dist)
            if dist == 4:
                src[...] = own_sum[16 * direction : 16 * (direction + 1)].astype(src.dtype)
            else:
                _, arrived, before = hop(w, 2, direction, dist + 1)
                total = crossed(w, far(direction, dist))
                before.wait_recv()
                if dist == 3:
                    low, high = total[:16], total[16:]
                    if direction == 0:
                        low = low + arrived[...].astype(f32)
                    else:
                        high = high + arrived[...].astype(f32)
                    src[0:16] = low.astype(src.dtype)
                    src[16:PART] = high.astype(src.dtype)
                else:
                    src[...] = (total + arrived[...].astype(f32)).astype(src.dtype)
            go(copy)

    def last_hops(w, lane, total):
        for direction in range(2):
            _, arrived, copy = hop(w, lane, direction, 1)
            copy.wait_recv()
            total = total + arrived[...]
        return total

    def swap_copy(w):
        return remote(x_out.at[w], x_in.at[w], ysend.at[w], yrecv.at[w], place.across)

    def turn(w):
        x_out[w] = last_hops(w, 1, summed(w, 0, 1, 1))
        go(swap_copy(w))

    def finish(w):
        total = last_hops(w, 2, crossed(w, 0))
        update[w, 0:PART, :] = rate_rows[w, 0:PART, :] * total
        total = last_hops(w, 0, summed(w, 0, 0, 1))
        swap_copy(w).wait_recv()
        total = total + x_in[w]
        update[w, PART:ROWS, :] = rate_rows[w, PART:ROWS, :] * total[0 : ROWS - PART]

    def scatter(w):
        cross(w, 4, 3, 5)
        ring_z(w, 4)
        yield 1
        cross(w, 2, 6)
        yield 2
        ring_z(w, 3)
        yield 3
        ring_x(w, 4)
        cross(w, 1, 7, 0)
        yield 4
        ring_z(w, 2)
        ring_x(w, 3)
        yield 5
        ring_z(w, 1)
        ring_x(w, 2)
        yield 6
        turn(w)
        yield 7
        ring_x(w, 1)
        yield 8
        finish(w)
        yield 9

    def rows(index, size=UNIT):
        return pl.ds(index * size, size)

    def fold(values):
        return values.reshape(values.shape[0] // 8, 8, C).sum(axis=0)

    def spread(sums):
        column = sums.sum(axis=0, keepdims=True)
        top = column.astype(bf16)
        rest = column - top.astype(f32)
        middle = rest.astype(bf16)
        low = (rest - middle.astype(f32)).astype(bf16)
        terms = jnp.concatenate([top, middle, low, jnp.zeros((13, C), bf16)], axis=0)
        total = jnp.dot(terms, same_group[...], preferred_element_type=f32)
        return total.sum(axis=0, keepdims=True) * (1.0 / (POINTS * PER_GROUP))

    def sweep(body, start):
        return lax.fori_loop(0, FRAMES, lambda i, carry: body(pl.ds(pl.multiple_of(i * HW, HW), HW), carry), start)

    def padded(i):
        return pl.ds(HW + i * UNIT, UNIT)

    def silu(v):
        return v / (1.0 + jnp.exp(-v))

    loads[0].wait()
    centre = spread(sweep(lambda at, acc: acc + fold(clip[at, :].astype(f32)), zero))

    def squares(ref, mean):
        def body(at, acc):
            off = ref[at, :].astype(f32) - mean
            return acc + fold(off * off)

        return lax.rsqrt(spread(sweep(body, zero)) + 1e-05)

    inverse = squares(clip, centre)
    units = POINTS // UNIT

    def act_unit(i):
        values = (clip[rows(i), :].astype(f32) - centre) * inverse
        act_one[padded(i), :] = silu(values).astype(bf16)

    def flip_unit(flipped, ref, i):
        flipped[:, rows(i)] = ref[padded(i), :].T

    ring_start(0)
    group_send(1)
    loads[2].start()
    for i in range(4):
        act_unit(i)
    ring_step(0, 1)
    ring_start(1)
    act_unit(4)
    act_unit(5)
    ring_step(0, 2)
    ring_step(1, 1)
    act_unit(6)
    ring_sides(0, 1)
    loads[1].wait()
    half_width = freqs.shape[1]
    angles = t_ref[0].astype(f32) * freqs[...]
    person = table[pl.ds(ident_ref[0], 1), :]
    embedding = jnp.concatenate([jnp.cos(angles), jnp.sin(angles)], axis=1) + person
    embed = jnp.broadcast_to(silu(embedding).astype(bf16), (16, 2 * half_width))
    bias = jnp.dot(embed, proj[...], preferred_element_type=f32)[0:1]
    ring_step(0, 3)
    ring_step(1, 2)
    for i in range(3):
        flip_unit(flip_one, act_one, i)
    ring_sides(0, 2)
    ring_step(0, 4)
    ring_step(1, 3)
    ring_sides(1, 1)
    for i in range(3, units):
        flip_unit(flip_one, act_one, i)
    ring_sides(0, 3)
    ring_sides(0, 4)
    ring_step(1, 4)
    ring_sides(1, 2)
    dense(0)

    def stacked(ref, start, size, taps):
        return jnp.concatenate([ref[pl.ds(start + HW * tap, size), :] for tap in taps], axis=1)

    half = POINTS // 2
    sums = zero
    for part in range(2):
        mixed = jnp.dot(stacked(act_one, part * half, half, (0, 1, 2)), weights[0], preferred_element_type=f32)
        values = SCALE * mixed + bias
        hid[pl.ds(part * half, half), :] = values
        sums = sums + fold(values)
        ring_sides(1, 3 + part)
    for step in range(1, N_GROUP):
        go(rate_copy(step, True))
    centre_two = spread(sums)
    inverse_two = squares(hid, centre_two)
    for i in range(units):
        values = (hid[rows(i), :] - centre_two) * inverse_two
        hid[rows(i), :] = values
        act_two[padded(i), :] = silu(values).astype(bf16)
    for i in range(units):
        flip_unit(flip_two, act_two, i)
    dense(1)
    loads[2].wait()

    for part in range(2):
        at = pl.ds(part * half, half)
        mixed = jnp.dot(stacked(act_two, part * half, half, (0, 1, 2)), weights[1], preferred_element_type=f32)
        output = clip[at, :].astype(f32) + SCALE * mixed
        err[pl.ds(HW + part * half, half), :] = (output - target[at, :].astype(f32)).astype(bf16)

    def weight_grad(flipped, ref, tap):
        grad[C * tap : C * (tap + 1), :] = jnp.dot(
            flipped[...], ref[pl.ds(HW * (2 - tap), POINTS), :], preferred_element_type=f32
        )

    for tap in range(3):
        weight_grad(flip_two, err, tap)
    lay(1)
    pair(1)

    scatter_two = scatter(1)
    sum_grad, sum_mixed = zero, zero
    for part in range(2):
        at = pl.ds(part * half, half)
        back = jnp.zeros((half, C), f32)
        for tap in range(3):
            back = back + lax.dot_general(
                err[pl.ds(part * half + HW * (2 - tap), half), :],
                weights[1, C * tap : C * (tap + 1), :],
                (((1,), (1,)), ((), ())),
                preferred_element_type=f32,
            )
        values = hid[at, :]
        gate = 1.0 / (1.0 + jnp.exp(-values))
        inner = (SCALE * back) * (gate * (1.0 + values * (1.0 - gate)))
        grad[at, :] = inner
        sum_grad = sum_grad + fold(inner)
        sum_mixed = sum_mixed + fold(inner * values)
        next(scatter_two)
        if part:
            next(scatter_two)
    mean_grad, mean_mixed = spread(sum_grad), spread(sum_mixed)
    for i in range(units):
        inner = grad[rows(i), :] - mean_grad - hid[rows(i), :] * mean_mixed
        grad_hid[padded(i), :] = (inner * inverse_two).astype(bf16)
    next(scatter_two)
    for tap in range(3):
        weight_grad(flip_one, grad_hid, tap)
        if tap == 1:
            next(scatter_two)
    lay(0)
    pair(0)
    scatter_one = scatter(0)
    next(scatter_one)
    next(scatter_one)
    next(scatter_two)
    for _ in range(3):
        next(scatter_one)
    for step in range(1, N_GROUP):
        rate_copy(step, False).wait_recv()
    for w in range(2):
        rate_rows[w] = assemble(lambda group: rbuf[w, group]) * SCALE
    next(scatter_two)
    next(scatter_two)
    next(scatter_one)
    next(scatter_two)
    for _ in range(3):
        next(scatter_one)
    for copy in sends:
        copy.wait_send()


def step(timestep, identity, freqs, table, clip, target, time_proj, w1, w2, r1, r2):
    f32, bf16 = jnp.float32, jnp.bfloat16
    dma = pltpu.SemaphoreType.DMA
    vmem = pl.BlockSpec(memory_space=pltpu.VMEM)
    smem = pl.BlockSpec(memory_space=pltpu.SMEM)
    anywhere = pl.BlockSpec(memory_space=pl.ANY)
    part = (PART, C)
    wide = (POINTS + 2 * HW, C)
    rows = jax.ShapeDtypeStruct((2, ROWS, C), f32)
    return pl.pallas_call(
        step_kernel,
        out_shape=(rows, rows),
        in_specs=[smem] * 2 + [vmem] * 2 + [anywhere] * 3 + [vmem] * 4,
        out_specs=(vmem,) * 2,
        scratch_shapes=[
            pltpu.VMEM((POINTS, C), bf16),
            pltpu.VMEM((POINTS, C), bf16),
            pltpu.VMEM(time_proj.shape, bf16),
            pltpu.VMEM((C, C), bf16),
            pltpu.VMEM(wide, bf16),
            pltpu.VMEM(wide, bf16),
            pltpu.VMEM(wide, bf16),
            pltpu.VMEM(wide, bf16),
            pltpu.VMEM((C, POINTS), bf16),
            pltpu.VMEM((C, POINTS), bf16),
            pltpu.VMEM((POINTS, C), f32),
            pltpu.VMEM((2, TAPS, C), bf16),
            pltpu.VMEM((TAPS + 8, C), f32),
            pltpu.VMEM((2, NX, N_GROUP, ROWS, COLS), bf16),
            pltpu.VMEM((2, N_GROUP, ROWS, COLS), bf16),
            pltpu.VMEM((2, NZ, NC, NX, 4, 16, C), bf16),
            pltpu.VMEM((2, NX, NZ, NC, 2) + part, f32),
            pltpu.VMEM((2, NZ, 2, 2) + part, f32),
            pltpu.VMEM((2, NZ) + part, bf16),
            pltpu.VMEM((2, NZ) + part, bf16),
            pltpu.VMEM((2, 2, 3, 3) + part, bf16),
            pltpu.VMEM((2, 2, 3, 3) + part, bf16),
            pltpu.VMEM((2, 2, 3) + part, f32),
            pltpu.VMEM((2, 2, 3) + part, f32),
            pltpu.VMEM((2,) + part, f32),
            pltpu.VMEM((2,) + part, f32),
            pltpu.VMEM((2, ROWS, C), f32),
            dma((3,)),
            dma((2, 2, N_GROUP)),
            dma((2, 2, N_GROUP)),
            dma((N_GROUP,)),
            dma((N_GROUP,)),
            dma((2, 2, 5, 2)),
            dma((2, 2, 5, 2)),
            dma((2, 2, NZ)),
            dma((2, 2, NZ)),
            dma((2, 2, NZ)),
            dma((2, 2, NZ)),
            dma((2, 2)),
            dma((2, 2)),
            dma((2, 3, 2, 5)),
            dma((2, 3, 2, 5)),
            dma((2,)),
            dma((2,)),
            dma((2, NZ, 2)),
            dma((2, NZ, 2)),
            dma((2, NZ)),
            dma((2, NZ)),
        ],
        compiler_params=pltpu.CompilerParams(
            collective_id=0, has_side_effects=True, vmem_limit_bytes=62 << 20
        ),
        name="inner_step",
    )(timestep, identity, freqs, table, clip, target, time_proj, w1, w2, r1, r2)


def shards(
    clips,
    targets,
    timestep,
    identity,
    conv1_weight,
    conv2_weight,
    rate1,
    rate2,
    time_proj,
    subject_table,
):
    half_width = subject_table.shape[1] // 2
    freqs = np.exp(-math.log(10000.0) * np.arange(half_width) / half_width).astype(np.float32)
    update, kept = step(
        timestep,
        identity,
        freqs[None],
        subject_table,
        clips.reshape(POINTS, C),
        targets.reshape(POINTS, C),
        time_proj,
        conv1_weight,
        conv2_weight,
        rate1,
        rate2,
    )
    return tuple((kept[w] - update[w])[None] for w in range(2))


def solution(mesh):
    return jax.shard_map(
        shards,
        mesh=mesh,
        in_specs=(
            P(("group", "member"), None, None, None),
            P(("group", "member"), None, None, None),
            P(("group", "member")),
            P(("group", "member")),
            P("member", "group"),
            P("member", "group"),
            P("member", "group"),
            P("member", "group"),
            P(),
            P(),
        ),
        out_specs=(P("group", "member", None), P("group", "member", None)),
        check_vma=False,
    )
```

```python
import functools
import math

import jax
import jax.numpy as jnp
import numpy as np
from jax import lax
from jax.experimental import pallas as pl
from jax.experimental.pallas import tpu as pltpu
from jax.sharding import PartitionSpec as P

GN_GROUPS = 32
MESH = pl.DeviceIdType.MESH
N_GROUP, N_MEMBER, NZ, NC, NX = 8, 32, 8, 2, 2
ROWS, COLS, C = 60, 80, 640
TAPS = 3 * C
FRAMES, HW = 14, 64
POINTS = FRAMES * HW
PER_GROUP = C // GN_GROUPS
SCALE = 1.0 / math.sqrt(TAPS)
UNIT = 128
PART = 32


class Place:
    def __init__(self):
        self.g = lax.axis_index("group")
        self.m = lax.axis_index("member")
        self.core = lax.rem(self.m, 2)
        self.q = lax.div(self.m, 2)
        self.z = lax.rem(self.q, NZ)
        self.xh = lax.div(self.q, NZ)
        self.up = self.at(self.xh, self.zof(1), self.core)
        self.down = self.at(self.xh, self.zof(-1), self.core)
        self.across = self.at(1 - self.xh, self.z, self.core)
        self.sibling = self.at(self.xh, self.z, 1 - self.core)
        self.x_lo = lax.rem(self.g, 2)
        self.y_lo = lax.rem(lax.div(self.g, 2), 2)
        self.beside_x = (self.g + 1 - 2 * self.x_lo, self.m)
        self.beside_y = (self.g + 2 - 4 * self.y_lo, self.m)
        self.opposite = self.across[1]
        self.twin = self.sibling[1]

    def at(self, xh, z, core):
        return (self.g, (xh * NZ + z) * 2 + core)

    def zof(self, step):
        return lax.rem(self.z + (step + NZ), NZ)

    def peer(self, step):
        return lax.rem(self.g + step, N_GROUP)

    def xof(self, piece):
        return self.xh if piece == 0 else 1 - self.xh


def remote(src, dst, send, recv, device):
    return pltpu.make_async_remote_copy(
        src_ref=src, dst_ref=dst, send_sem=send, recv_sem=recv, device_id=device, device_id_type=MESH
    )


def partners(place):
    plane = [((place.peer(step), place.m)) for step in range(1, N_GROUP)]
    beyond = [((place.peer(step), place.opposite)) for step in range(N_GROUP)]
    sides = [(place.beside_x[0], place.twin), (place.beside_y[0], place.twin)]
    return plane + beyond + sides + [place.up, place.down, place.sibling]


def exists(direction, dist, piece):
    return dist < 4 or (dist == 4 and piece == direction)


def step_kernel(
    t_ref, ident_ref, freqs, table, clip_hbm, target_hbm, proj_hbm, w1, w2, r1, r2, update, kept,
    clip, target, proj, same_group, act_one, act_two, err, grad_hid, flip_one, flip_two, hid, weights, grad,
    gbuf, rbuf, wbuf, blocks, sib_in, cross_out, cross_in, hop_out, hop_in, near_out, last_in, x_out, x_in, rate_rows,
    load_sem, gsend, grecv, rate_send, rate_recv, zsend, zrecv, ssend, srecv, bsend, brecv, tsend, trecv,
    rsend, rrecv, ysend, yrecv, psend, precv, csend, crecv,
):
    f32, bf16 = jnp.float32, jnp.bfloat16
    place = Place()
    sends = []

    def go(copy):
        copy.start()
        sends.append(copy)

    def settle(count):
        for copy in sends[:count]:
            copy.wait_send()
        del sends[:count]

    barrier = pltpu.get_barrier_semaphore()
    friends = partners(place)
    for friend in friends:
        pl.semaphore_signal(barrier, inc=1, device_id=friend, device_id_type=MESH)
    for index, ref in enumerate((w1, w2)):
        gbuf[index, 0, place.g] = ref[...]
    for index, ref in enumerate((r1, r2)):
        rbuf[index, place.g] = ref[...]
    first = lax.broadcasted_iota(jnp.int32, (C, C), 0)
    second = lax.broadcasted_iota(jnp.int32, (C, C), 1)
    same_group[...] = (((first * 3277) >> 16) == ((second * 3277) >> 16)).astype(f32).astype(bf16)
    blank = jnp.zeros((HW, C), bf16)
    for ref in (act_one, act_two, err, grad_hid):
        ref[0:HW, :] = blank
        ref[HW + POINTS :, :] = blank
    zero = jnp.zeros((8, C), f32)
    grad[TAPS:, :] = zero
    pl.semaphore_wait(barrier, len(friends))

    def group_copy(w, beyond, step, here):
        source = place.g if here else lax.rem(place.g + (N_GROUP - step), N_GROUP)
        to = (place.peer(step), place.opposite if beyond else place.m)
        at = (w, beyond, step)
        return remote(gbuf.at[w, 0, source if not beyond else place.g], gbuf.at[w, beyond, source],
                      gsend.at[at], grecv.at[at], to)

    def group_send(w):
        for beyond in range(2):
            for step in range(1 - beyond, N_GROUP):
                go(group_copy(w, beyond, step, True))

    def rate_copy(step, here):
        source = place.g if here else lax.rem(place.g + (N_GROUP - step), N_GROUP)
        ref = rbuf.at[:, source]
        return remote(ref, ref, rate_send.at[step], rate_recv.at[step], (place.peer(step), place.m))

    group_send(0)
    loads = [
        pltpu.make_async_copy(src, dst, load_sem.at[i])
        for i, (src, dst) in enumerate(((clip_hbm, clip), (proj_hbm, proj), (target_hbm, target)))
    ]
    loads[0].start()
    loads[1].start()

    def assemble(read):
        return jnp.concatenate([read(group).astype(f32) for group in range(N_GROUP)], axis=1)

    tile_slot = (2 * place.x_lo, 2 - 2 * place.x_lo, 1 + 2 * place.y_lo, 3 - 2 * place.y_lo)

    def slot(w, dist, piece, first, count):
        return wbuf.at[w, place.zof(-dist), place.core, place.xof(piece), pl.ds(first, count)]

    def slots(w, dist, first, count, core=None):
        core = place.core if core is None else core
        return wbuf.at[w, place.zof(-dist), core, :, pl.ds(first, count)]

    def share_copy(w, dist, high, count, here):
        ref = slots(w, dist, 2 * high, count, place.core if here else 1 - place.core)
        at = (w, high, dist % NZ)
        return remote(ref, ref, ssend.at[at], srecv.at[at], place.sibling)

    def side_copy(w, side, dist):
        src, dst = slots(w, dist, side, 1), slots(w, dist, side + 2, 1)
        at = (w, side, dist % NZ)
        return remote(src, dst, bsend.at[at], brecv.at[at], (place.beside_x, place.beside_y)[side])

    def ring_copy(w, direction, dist, piece, here):
        sign = 1 if direction == 0 else -1
        ref = slot(w, sign * (dist - 1 if here else dist), piece, 0, 2)
        to = place.up if direction == 0 else place.down
        return remote(ref, ref, zsend.at[w, direction, dist, piece], zrecv.at[w, direction, dist, piece], to)

    def forward(w, direction, dist, piece):
        if exists(direction, dist, piece):
            go(ring_copy(w, direction, dist, piece, True))

    def end_copy(w, side):
        src, dst = slots(w, 4, side, 1), slots(w, 4, side + 2, 1)
        to = ((place.beside_x, place.beside_y)[side][0], place.twin)
        return remote(src, dst, tsend.at[w, side], trecv.at[w, side], to)

    def end_in(w, side):
        ref = slots(w, 4, side + 2, 1, 1 - place.core)
        return remote(ref, ref, tsend.at[w, side], trecv.at[w, side], place.sibling)

    def hand_on(w, dist):
        for side in range(2):
            go(side_copy(w, side, dist))
            if dist == 4:
                go(end_copy(w, side))
        go(share_copy(w, dist, 0, 2, True))

    def plane_block(w, piece):
        for step in range(1 - piece, N_GROUP):
            group_copy(w, piece, step, False).wait_recv()
        rows_f32 = assemble(lambda group: gbuf[w, piece, group])
        whole = jnp.concatenate([rows_f32, jnp.zeros((4, C), f32)], axis=0).astype(bf16)
        if piece == 0:
            kept[w, :, 0, :] = rows_f32
        for tile in range(4):
            wbuf[w, place.z, place.core, place.xof(piece), tile_slot[tile]] = whole[16 * tile : 16 * (tile + 1)]
        for direction in range(2):
            forward(w, direction, 1, piece)

    def ring_start(w):
        for piece in range(2):
            plane_block(w, piece)
        go(share_copy(w, 0, 0, 4, True))

    def ring_step(w, dist):
        for piece in range(2):
            for direction in range(2):
                if exists(direction, dist, piece):
                    ring_copy(w, direction, dist, piece, False).wait_recv()
                    forward(w, direction, dist + 1, piece)
        for far in sorted({dist, NZ - dist}):
            hand_on(w, far)

    def ring_sides(w, dist):
        for far in sorted({dist, NZ - dist}):
            for side in range(2):
                side_copy(w, side, far).wait_recv()
            if dist < 4:
                go(share_copy(w, far, 1, 2, True))

    def dense(w):
        for dist in range(NZ):
            share_copy(w, dist, 0, 2 if dist else 4, False).wait_recv()
            if dist == 4:
                for side in range(2):
                    end_in(w, side).wait_recv()
            elif dist:
                share_copy(w, dist, 1, 2, False).wait_recv()
        for m in range(N_MEMBER):
            for tile in range(4):
                start, size = ROWS * m + 16 * tile, min(16, ROWS - 16 * tile)
                block = wbuf[w, (m // 2) % NZ, m % 2, m // 16, tile_slot[tile]]
                weights[w, start : start + size, :] = block[0:size]

    def pair_copy(w, xh, z):
        src = blocks.at[w, xh, z, 1 - place.core]
        dst = sib_in.at[w, xh, z]
        return remote(src, dst, psend.at[w, xh, z], precv.at[w, xh, z], place.sibling)

    def pair(w, first, last):
        for q in range(first, last):
            for m in (2 * q, 2 * q + 1):
                for part in range(2):
                    start = ROWS * m + PART * part
                    blocks[w, q // NZ, q % NZ, m % 2, part] = grad[start : start + PART, :]
            go(pair_copy(w, q // NZ, q % NZ))

    paired = set()

    def summed(w, dist, piece, part):
        at = (place.xof(piece), place.zof(dist))
        if (w, dist, piece) not in paired:
            paired.add((w, dist, piece))
            pair_copy(w, *at).wait_recv()
        return blocks[w, at[0], at[1], place.core, part] + sib_in[w, at[0], at[1], part]

    def cross_copy(w, dist):
        at = (w, dist)
        return remote(cross_out.at[at], cross_in.at[at], csend.at[at], crecv.at[at], place.across)

    def cross(w, *dists):
        for dist in dists:
            cross_out[w, dist] = summed(w, dist, 1, 0).astype(bf16)
            go(cross_copy(w, dist))

    def crossed(w, dist):
        cross_copy(w, dist).wait_recv()
        return summed(w, dist, 0, 0) + cross_in[w, dist].astype(f32)

    def merges(lane, direction):
        return lane < 2 and direction != lane

    def hop(w, lane, direction, dist):
        at = (w, lane, direction, dist)
        to = place.up if direction == 0 else place.down
        if dist == 1:
            src = near_out.at[w, direction, lane] if merges(lane, direction) else hop_in.at[w, direction, 0, lane]
            dst = last_in.at[w, direction, 0, lane]
        elif dist == 0:
            src, dst = near_out.at[w, direction, lane], last_in.at[w, direction, 1, lane]
        else:
            src, dst = hop_out.at[w, direction, dist - 2, lane], hop_in.at[w, direction, dist - 2, lane]
        if lane == 2 and dist == 4:
            src, dst = src.at[pl.ds(16 * direction, 16)], dst.at[pl.ds(16 * direction, 16)]
        return src, dst, remote(src, dst, rsend.at[at], rrecv.at[at], to)

    def far(direction, dist):
        return dist if direction == 0 else NZ - dist

    def near_z(w):
        for piece in (1, 0):
            src, _, copy = hop(w, piece, piece, 0)
            src[...] = summed(w, far(piece, 1), piece, 1).astype(bf16)
            go(copy)

    def near_x(w):
        for direction in range(2):
            src, _, copy = hop(w, 2, direction, 0)
            src[...] = crossed(w, far(direction, 1)).astype(bf16)
            go(copy)

    def pass_on(w, lane):
        for direction in range(2):
            _, arrived, before = hop(w, lane, direction, 2)
            before.wait_recv()
            src, _, copy = hop(w, lane, direction, 1)
            if merges(lane, direction):
                src[...] = (summed(w, far(direction, 1), lane, 1) + arrived[...].astype(f32)).astype(bf16)
            go(copy)

    def ring_z(w, dist):
        for piece in (1, 0):
            for direction in range(2):
                if not exists(direction, dist, piece):
                    continue
                total = summed(w, far(direction, dist), piece, 1)
                if exists(direction, dist + 1, piece):
                    _, arrived, copy = hop(w, piece, direction, dist + 1)
                    copy.wait_recv()
                    total = total + arrived[...].astype(f32)
                src, _, copy = hop(w, piece, direction, dist)
                src[...] = total.astype(src.dtype)
                go(copy)

    def ring_x(w, dist):
        own_sum = crossed(w, 4) if dist == 4 else None
        for direction in range(2):
            src, _, copy = hop(w, 2, direction, dist)
            if dist == 4:
                src[...] = own_sum[16 * direction : 16 * (direction + 1)].astype(src.dtype)
            else:
                _, arrived, before = hop(w, 2, direction, dist + 1)
                total = crossed(w, far(direction, dist))
                before.wait_recv()
                if dist == 3:
                    low, high = total[:16], total[16:]
                    if direction == 0:
                        low = low + arrived[...].astype(f32)
                    else:
                        high = high + arrived[...].astype(f32)
                    src[0:16] = low.astype(src.dtype)
                    src[16:PART] = high.astype(src.dtype)
                else:
                    src[...] = (total + arrived[...].astype(f32)).astype(src.dtype)
            go(copy)

    def last_hops(w, lane, total):
        for direction in range(2):
            for dist in (1,) if merges(lane, direction) else (0, 1):
                _, arrived, copy = hop(w, lane, direction, dist)
                copy.wait_recv()
                total = total + arrived[...].astype(f32)
        return total

    def swap_copy(w):
        return remote(x_out.at[w], x_in.at[w], ysend.at[w], yrecv.at[w], place.across)

    def turn(w):
        x_out[w] = last_hops(w, 1, summed(w, 0, 1, 1))
        go(swap_copy(w))

    def finish(w):
        total = last_hops(w, 2, crossed(w, 0))
        update[w, 0:PART, 0, :] = rate_rows[w, 0:PART, :] * total
        total = last_hops(w, 0, summed(w, 0, 0, 1))
        swap_copy(w).wait_recv()
        total = total + x_in[w]
        update[w, PART:ROWS, 0, :] = rate_rows[w, PART:ROWS, :] * total[0 : ROWS - PART]

    def scatter(w):
        cross(w, 4, 3, 5)
        ring_z(w, 4)
        yield 1
        cross(w, 2, 6)
        near_z(w)
        yield 2
        ring_z(w, 3)
        yield 3
        ring_x(w, 4)
        cross(w, 1, 7, 0)
        yield 4
        ring_z(w, 2)
        ring_x(w, 3)
        yield 5
        near_x(w)
        pass_on(w, 1)
        pass_on(w, 0)
        ring_x(w, 2)
        yield 6
        turn(w)
        yield 7
        pass_on(w, 2)
        yield 8
        finish(w)
        yield 9

    def rows(index, size=UNIT):
        return pl.ds(index * size, size)

    def fold(values):
        return values.reshape(values.shape[0] // 8, 8, C).sum(axis=0)

    def spread(sums):
        column = sums.sum(axis=0, keepdims=True)
        top = column.astype(bf16)
        rest = column - top.astype(f32)
        middle = rest.astype(bf16)
        low = (rest - middle.astype(f32)).astype(bf16)
        terms = jnp.concatenate([top, middle, low, jnp.zeros((13, C), bf16)], axis=0)
        total = jnp.dot(terms, same_group[...], preferred_element_type=f32)
        return total.sum(axis=0, keepdims=True) * (1.0 / (POINTS * PER_GROUP))

    def sweep(body, start):
        return lax.fori_loop(0, FRAMES, lambda i, carry: body(pl.ds(pl.multiple_of(i * HW, HW), HW), carry), start)

    def padded(i):
        return pl.ds(HW + i * UNIT, UNIT)

    def silu(v):
        return v / (1.0 + jnp.exp(-v))

    loads[0].wait()
    centre = spread(sweep(lambda at, acc: acc + fold(clip[at, :].astype(f32)), zero))

    def squares(ref, mean):
        def body(at, acc):
            off = ref[at, :].astype(f32) - mean
            return acc + fold(off * off)

        return lax.rsqrt(spread(sweep(body, zero)) + 1e-05)

    inverse = squares(clip, centre)
    units = POINTS // UNIT

    def act_unit(i):
        values = (clip[rows(i), :].astype(f32) - centre) * inverse
        act_one[padded(i), :] = silu(values).astype(bf16)

    def flip_unit(flipped, ref, i):
        flipped[:, rows(i)] = ref[padded(i), :].T

    ring_start(0)
    group_send(1)
    loads[2].start()
    for i in range(4):
        act_unit(i)
    ring_step(0, 1)
    ring_start(1)
    act_unit(4)
    act_unit(5)
    ring_step(0, 2)
    ring_step(1, 1)
    act_unit(6)
    ring_sides(0, 1)
    loads[1].wait()
    half_width = freqs.shape[1]
    angles = t_ref[0].astype(f32) * freqs[...]
    person = table[pl.ds(ident_ref[0], 1), :]
    embedding = jnp.concatenate([jnp.cos(angles), jnp.sin(angles)], axis=1) + person
    embed = jnp.broadcast_to(silu(embedding).astype(bf16), (16, 2 * half_width))
    bias = jnp.dot(embed, proj[...], preferred_element_type=f32)[0:1]
    ring_step(0, 3)
    ring_step(1, 2)
    for i in range(3):
        flip_unit(flip_one, act_one, i)
    ring_sides(0, 2)
    ring_step(0, 4)
    ring_step(1, 3)
    ring_sides(1, 1)
    for i in range(3, units):
        flip_unit(flip_one, act_one, i)
    ring_sides(0, 3)
    ring_sides(0, 4)
    ring_step(1, 4)
    ring_sides(1, 2)
    dense(0)

    def stacked(ref, start, size, taps):
        return jnp.concatenate([ref[pl.ds(start + HW * tap, size), :] for tap in taps], axis=1)

    half = POINTS // 2
    sums = zero
    for part in range(2):
        mixed = jnp.dot(stacked(act_one, part * half, half, (0, 1, 2)), weights[0], preferred_element_type=f32)
        values = SCALE * mixed + bias
        hid[pl.ds(part * half, half), :] = values
        sums = sums + fold(values)
        ring_sides(1, 3 + part)
    for step in range(1, N_GROUP):
        go(rate_copy(step, True))
    centre_two = spread(sums)
    inverse_two = squares(hid, centre_two)
    for i in range(units):
        values = (hid[rows(i), :] - centre_two) * inverse_two
        hid[rows(i), :] = values
        act_two[padded(i), :] = silu(values).astype(bf16)
    for i in range(units):
        flip_unit(flip_two, act_two, i)
    dense(1)
    loads[2].wait()

    for part in range(2):
        at = pl.ds(part * half, half)
        mixed = jnp.dot(stacked(act_two, part * half, half, (0, 1, 2)), weights[1], preferred_element_type=f32)
        output = clip[at, :].astype(f32) + SCALE * mixed
        err[pl.ds(HW + part * half, half), :] = (output - target[at, :].astype(f32)).astype(bf16)

    def weight_grad(flipped, ref, tap):
        grad[C * tap : C * (tap + 1), :] = jnp.dot(
            flipped[...], ref[pl.ds(HW * (2 - tap), POINTS), :], preferred_element_type=f32
        )

    ready = (0, 5, 10, 16)
    for tap in range(3):
        weight_grad(flip_two, err, tap)
        pair(1, ready[tap], ready[tap + 1])

    scatter_two = scatter(1)
    sum_grad, sum_mixed = zero, zero
    for part in range(2):
        at = pl.ds(part * half, half)
        back = jnp.zeros((half, C), f32)
        for tap in range(3):
            back = back + lax.dot_general(
                err[pl.ds(part * half + HW * (2 - tap), half), :],
                weights[1, C * tap : C * (tap + 1), :],
                (((1,), (1,)), ((), ())),
                preferred_element_type=f32,
            )
        values = hid[at, :]
        gate = 1.0 / (1.0 + jnp.exp(-values))
        inner = (SCALE * back) * (gate * (1.0 + values * (1.0 - gate)))
        grad[at, :] = inner
        sum_grad = sum_grad + fold(inner)
        sum_mixed = sum_mixed + fold(inner * values)
        next(scatter_two)
        if part:
            next(scatter_two)
    mean_grad, mean_mixed = spread(sum_grad), spread(sum_mixed)
    for i in range(units):
        inner = grad[rows(i), :] - mean_grad - hid[rows(i), :] * mean_mixed
        grad_hid[padded(i), :] = (inner * inverse_two).astype(bf16)
    next(scatter_two)
    for tap in range(3):
        weight_grad(flip_one, grad_hid, tap)
        pair(0, ready[tap], ready[tap + 1])
        if tap == 1:
            next(scatter_two)
    scatter_one = scatter(0)
    early = 28
    next(scatter_one)
    next(scatter_one)
    settle(early)
    next(scatter_two)
    settle(early)
    next(scatter_one)
    settle(early)
    next(scatter_one)
    for step in range(1, N_GROUP):
        rate_copy(step, False).wait_recv()
    for w in range(2):
        rate_rows[w] = assemble(lambda group: rbuf[w, group]) * SCALE
    next(scatter_one)
    settle(early)
    next(scatter_two)
    next(scatter_two)
    settle(early)
    next(scatter_one)
    next(scatter_two)
    settle(early)
    next(scatter_one)
    settle(early)
    next(scatter_one)
    settle(early // 2)
    next(scatter_one)
    settle(len(sends))


def step(timestep, identity, freqs, table, clip, target, time_proj, w1, w2, r1, r2):
    f32, bf16 = jnp.float32, jnp.bfloat16
    dma = pltpu.SemaphoreType.DMA
    vmem = pl.BlockSpec(memory_space=pltpu.VMEM)
    smem = pl.BlockSpec(memory_space=pltpu.SMEM)
    anywhere = pl.BlockSpec(memory_space=pl.ANY)
    part = (PART, C)
    wide = (POINTS + 2 * HW, C)
    rows = jax.ShapeDtypeStruct((2, ROWS, 1, C), f32)
    return pl.pallas_call(
        step_kernel,
        out_shape=(rows, rows),
        in_specs=[smem] * 2 + [vmem] * 2 + [anywhere] * 3 + [vmem] * 4,
        out_specs=(vmem,) * 2,
        scratch_shapes=[
            pltpu.VMEM((POINTS, C), bf16),
            pltpu.VMEM((POINTS, C), bf16),
            pltpu.VMEM(time_proj.shape, bf16),
            pltpu.VMEM((C, C), bf16),
            pltpu.VMEM(wide, bf16),
            pltpu.VMEM(wide, bf16),
            pltpu.VMEM(wide, bf16),
            pltpu.VMEM(wide, bf16),
            pltpu.VMEM((C, POINTS), bf16),
            pltpu.VMEM((C, POINTS), bf16),
            pltpu.VMEM((POINTS, C), f32),
            pltpu.VMEM((2, TAPS, C), bf16),
            pltpu.VMEM((TAPS + 8, C), f32),
            pltpu.VMEM((2, NX, N_GROUP, ROWS, COLS), bf16),
            pltpu.VMEM((2, N_GROUP, ROWS, COLS), bf16),
            pltpu.VMEM((2, NZ, NC, NX, 4, 16, C), bf16),
            pltpu.VMEM((2, NX, NZ, NC, 2) + part, f32),
            pltpu.VMEM((2, NX, NZ, 2) + part, f32),
            pltpu.VMEM((2, NZ) + part, bf16),
            pltpu.VMEM((2, NZ) + part, bf16),
            pltpu.VMEM((2, 2, 3, 3) + part, bf16),
            pltpu.VMEM((2, 2, 3, 3) + part, bf16),
            pltpu.VMEM((2, 2, 3) + part, bf16),
            pltpu.VMEM((2, 2, 2, 3) + part, bf16),
            pltpu.VMEM((2,) + part, f32),
            pltpu.VMEM((2,) + part, f32),
            pltpu.VMEM((2, ROWS, C), f32),
            dma((3,)),
            dma((2, 2, N_GROUP)),
            dma((2, 2, N_GROUP)),
            dma((N_GROUP,)),
            dma((N_GROUP,)),
            dma((2, 2, 5, 2)),
            dma((2, 2, 5, 2)),
            dma((2, 2, NZ)),
            dma((2, 2, NZ)),
            dma((2, 2, NZ)),
            dma((2, 2, NZ)),
            dma((2, 2)),
            dma((2, 2)),
            dma((2, 3, 2, 5)),
            dma((2, 3, 2, 5)),
            dma((2,)),
            dma((2,)),
            dma((2, NX, NZ)),
            dma((2, NX, NZ)),
            dma((2, NZ)),
            dma((2, NZ)),
        ],
        compiler_params=pltpu.CompilerParams(
            collective_id=0, has_side_effects=True, vmem_limit_bytes=62 << 20
        ),
        name="inner_step",
    )(timestep, identity, freqs, table, clip, target, time_proj, w1, w2, r1, r2)


def shards(
    clips,
    targets,
    timestep,
    identity,
    conv1_weight,
    conv2_weight,
    rate1,
    rate2,
    time_proj,
    subject_table,
):
    half_width = subject_table.shape[1] // 2
    freqs = np.exp(-math.log(10000.0) * np.arange(half_width) / half_width).astype(np.float32)
    update, kept = step(
        timestep,
        identity,
        freqs[None],
        subject_table,
        clips.reshape(POINTS, C),
        targets.reshape(POINTS, C),
        time_proj,
        conv1_weight,
        conv2_weight,
        rate1,
        rate2,
    )
    return tuple((kept[w] - update[w]).transpose(1, 0, 2) for w in range(2))


def solution(mesh):
    return jax.shard_map(
        shards,
        mesh=mesh,
        in_specs=(
            P(("group", "member"), None, None, None),
            P(("group", "member"), None, None, None),
            P(("group", "member")),
            P(("group", "member")),
            P("member", "group"),
            P("member", "group"),
            P("member", "group"),
            P("member", "group"),
            P(),
            P(),
        ),
        out_specs=(P("group", "member", None), P("group", "member", None)),
        check_vma=False,
    )
```

```python
import functools
import math

import jax
import jax.numpy as jnp
import numpy as np
from jax import lax
from jax.experimental import pallas as pl
from jax.experimental.pallas import tpu as pltpu
from jax.sharding import PartitionSpec as P

GN_GROUPS = 32
MESH = pl.DeviceIdType.MESH
N_GROUP, N_MEMBER, NZ, NC, NX = 8, 32, 8, 2, 2
ROWS, COLS, C = 60, 80, 640
TAPS = 3 * C
FRAMES, HW = 14, 64
POINTS = FRAMES * HW
PER_GROUP = C // GN_GROUPS
SCALE = 1.0 / math.sqrt(TAPS)
UNIT = 128
PADDED = 64
CROSSED = (48, 32)


class Place:
    def __init__(self):
        self.g = lax.axis_index("group")
        self.m = lax.axis_index("member")
        self.core = lax.rem(self.m, 2)
        self.q = lax.div(self.m, 2)
        self.z = lax.rem(self.q, NZ)
        self.xh = lax.div(self.q, NZ)
        self.up = self.at(self.xh, self.zof(1), self.core)
        self.down = self.at(self.xh, self.zof(-1), self.core)
        self.across = self.at(1 - self.xh, self.z, self.core)
        self.sibling = self.at(self.xh, self.z, 1 - self.core)
        self.x_lo = lax.rem(self.g, 2)
        self.y_lo = lax.rem(lax.div(self.g, 2), 2)
        self.beside_x = (self.g + 1 - 2 * self.x_lo, self.m)
        self.beside_y = (self.g + 2 - 4 * self.y_lo, self.m)
        self.opposite = self.across[1]
        self.twin = self.sibling[1]

    def at(self, xh, z, core):
        return (self.g, (xh * NZ + z) * 2 + core)

    def zof(self, step):
        return lax.rem(self.z + (step + NZ), NZ)

    def peer(self, step):
        return lax.rem(self.g + step, N_GROUP)

    def xof(self, piece):
        return self.xh if piece == 0 else 1 - self.xh


def remote(src, dst, send, recv, device):
    return pltpu.make_async_remote_copy(
        src_ref=src, dst_ref=dst, send_sem=send, recv_sem=recv, device_id=device, device_id_type=MESH
    )


def partners(place):
    plane = [((place.peer(step), place.m)) for step in range(1, N_GROUP)]
    beyond = [((place.peer(step), place.opposite)) for step in range(N_GROUP)]
    sides = [(place.beside_x[0], place.twin), (place.beside_y[0], place.twin)]
    return plane + beyond + sides + [place.up, place.down, place.sibling]


def exists(direction, dist, piece):
    return dist < 4 or (dist == 4 and piece == direction)


def step_kernel(
    t_ref, ident_ref, freqs, table, clip_hbm, target_hbm, proj_hbm, w1, w2, r1, r2, update, kept,
    clip, target, proj, same_group, act_one, act_two, err, grad_hid, flip_one, flip_two, hid, weights, grad,
    gbuf, rbuf, wbuf, blocks, sib_in, cross_out, cross_in, hop_out, hop_in, near_out, last_in, x_out, x_in, rate_rows,
    load_sem, gsend, grecv, rate_send, rate_recv, zsend, zrecv, ssend, srecv, bsend, brecv, tsend, trecv,
    rsend, rrecv, ysend, yrecv, psend, precv, csend, crecv,
):
    f32, bf16 = jnp.float32, jnp.bfloat16
    place = Place()
    sends = []

    def go(copy):
        copy.start()
        sends.append(copy)

    def settle(count):
        for copy in sends[:count]:
            copy.wait_send()
        del sends[:count]

    barrier = pltpu.get_barrier_semaphore()
    friends = partners(place)
    for friend in friends:
        pl.semaphore_signal(barrier, inc=1, device_id=friend, device_id_type=MESH)
    for index, ref in enumerate((w1, w2)):
        gbuf[index, 0, place.g] = ref[...]
    for index, ref in enumerate((r1, r2)):
        rbuf[index, place.g] = ref[...]
    first = lax.broadcasted_iota(jnp.int32, (C, C), 0)
    second = lax.broadcasted_iota(jnp.int32, (C, C), 1)
    same_group[...] = (((first * 3277) >> 16) == ((second * 3277) >> 16)).astype(f32).astype(bf16)
    blank = jnp.zeros((HW, C), bf16)
    for ref in (act_one, act_two, err, grad_hid):
        ref[0:HW, :] = blank
        ref[HW + POINTS :, :] = blank
    zero = jnp.zeros((8, C), f32)
    grad[TAPS:, :] = zero
    pl.semaphore_wait(barrier, len(friends))

    def group_copy(w, beyond, step, here):
        source = place.g if here else lax.rem(place.g + (N_GROUP - step), N_GROUP)
        to = (place.peer(step), place.opposite if beyond else place.m)
        at = (w, beyond, step)
        return remote(gbuf.at[w, 0, source if not beyond else place.g], gbuf.at[w, beyond, source],
                      gsend.at[at], grecv.at[at], to)

    def group_send(w):
        for beyond in range(2):
            for step in range(1 - beyond, N_GROUP):
                go(group_copy(w, beyond, step, True))

    def rate_copy(step, here):
        source = place.g if here else lax.rem(place.g + (N_GROUP - step), N_GROUP)
        ref = rbuf.at[:, source]
        return remote(ref, ref, rate_send.at[step], rate_recv.at[step], (place.peer(step), place.m))

    group_send(0)
    loads = [
        pltpu.make_async_copy(src, dst, load_sem.at[i])
        for i, (src, dst) in enumerate(((clip_hbm, clip), (proj_hbm, proj), (target_hbm, target)))
    ]
    loads[0].start()
    loads[1].start()

    def assemble(read):
        return jnp.concatenate([read(group).astype(f32) for group in range(N_GROUP)], axis=1)

    tile_slot = (2 * place.x_lo, 2 - 2 * place.x_lo, 1 + 2 * place.y_lo, 3 - 2 * place.y_lo)

    def slot(w, dist, piece, first, count):
        return wbuf.at[w, place.zof(-dist), place.core, place.xof(piece), pl.ds(first, count)]

    def slots(w, dist, first, count, core=None):
        core = place.core if core is None else core
        return wbuf.at[w, place.zof(-dist), core, :, pl.ds(first, count)]

    def share_copy(w, dist, high, count, here):
        ref = slots(w, dist, 2 * high, count, place.core if here else 1 - place.core)
        at = (w, high, dist % NZ)
        return remote(ref, ref, ssend.at[at], srecv.at[at], place.sibling)

    def side_copy(w, side, dist):
        src, dst = slots(w, dist, side, 1), slots(w, dist, side + 2, 1)
        at = (w, side, dist % NZ)
        return remote(src, dst, bsend.at[at], brecv.at[at], (place.beside_x, place.beside_y)[side])

    def ring_copy(w, direction, dist, piece, here):
        sign = 1 if direction == 0 else -1
        ref = slot(w, sign * (dist - 1 if here else dist), piece, 0, 2)
        to = place.up if direction == 0 else place.down
        return remote(ref, ref, zsend.at[w, direction, dist, piece], zrecv.at[w, direction, dist, piece], to)

    def forward(w, direction, dist, piece):
        if exists(direction, dist, piece):
            go(ring_copy(w, direction, dist, piece, True))

    def end_copy(w, side):
        src, dst = slots(w, 4, side, 1), slots(w, 4, side + 2, 1)
        to = ((place.beside_x, place.beside_y)[side][0], place.twin)
        return remote(src, dst, tsend.at[w, side], trecv.at[w, side], to)

    def end_in(w, side):
        ref = slots(w, 4, side + 2, 1, 1 - place.core)
        return remote(ref, ref, tsend.at[w, side], trecv.at[w, side], place.sibling)

    def hand_on(w, dist):
        for side in range(2):
            go(side_copy(w, side, dist))
            if dist == 4:
                go(end_copy(w, side))
        go(share_copy(w, dist, 0, 2, True))

    def plane_block(w, piece):
        for step in range(1 - piece, N_GROUP):
            group_copy(w, piece, step, False).wait_recv()
        rows_f32 = assemble(lambda group: gbuf[w, piece, group])
        whole = jnp.concatenate([rows_f32, jnp.zeros((4, C), f32)], axis=0).astype(bf16)
        if piece == 0:
            kept[w, :, 0, :] = rows_f32
        for tile in range(4):
            wbuf[w, place.z, place.core, place.xof(piece), tile_slot[tile]] = whole[16 * tile : 16 * (tile + 1)]
        for direction in range(2):
            forward(w, direction, 1, piece)

    def ring_start(w):
        for piece in range(2):
            plane_block(w, piece)
        go(share_copy(w, 0, 0, 4, True))

    def ring_step(w, dist):
        for piece in range(2):
            for direction in range(2):
                if exists(direction, dist, piece):
                    ring_copy(w, direction, dist, piece, False).wait_recv()
                    forward(w, direction, dist + 1, piece)
        for far in sorted({dist, NZ - dist}):
            hand_on(w, far)

    def ring_sides(w, dist):
        for far in sorted({dist, NZ - dist}):
            for side in range(2):
                side_copy(w, side, far).wait_recv()
            if dist < 4:
                go(share_copy(w, far, 1, 2, True))

    def dense(w):
        for dist in range(NZ):
            share_copy(w, dist, 0, 2 if dist else 4, False).wait_recv()
            if dist == 4:
                for side in range(2):
                    end_in(w, side).wait_recv()
            elif dist:
                share_copy(w, dist, 1, 2, False).wait_recv()
        for m in range(N_MEMBER):
            for tile in range(4):
                start, size = ROWS * m + 16 * tile, min(16, ROWS - 16 * tile)
                block = wbuf[w, (m // 2) % NZ, m % 2, m // 16, tile_slot[tile]]
                weights[w, start : start + size, :] = block[0:size]

    def pair_copy(w, xh, z):
        src = blocks.at[w, xh, z, 1 - place.core]
        dst = sib_in.at[w, xh, z]
        return remote(src, dst, psend.at[w, xh, z], precv.at[w, xh, z], place.sibling)

    def pair(w, first, last):
        for q in range(first, last):
            for m in (2 * q, 2 * q + 1):
                blocks[w, q // NZ, q % NZ, m % 2] = grad[ROWS * m : ROWS * m + PADDED, :]
            go(pair_copy(w, q // NZ, q % NZ))

    paired = set()

    def summed(w, dist, piece, part):
        at = (place.xof(piece), place.zof(dist))
        if (w, dist, piece) not in paired:
            paired.add((w, dist, piece))
            pair_copy(w, *at).wait_recv()
        part_rows = pl.ds(0, CROSSED[w]) if part == 0 else pl.ds(CROSSED[w], PADDED - CROSSED[w])
        return blocks[w, at[0], at[1], place.core, part_rows] + sib_in[w, at[0], at[1], part_rows]

    def cross_copy(w, dist):
        at, span = (w, dist), pl.ds(0, CROSSED[w])
        return remote(cross_out.at[at].at[span], cross_in.at[at].at[span], csend.at[at], crecv.at[at], place.across)

    def cross(w, *dists):
        for dist in dists:
            cross_out[w, dist, 0 : CROSSED[w]] = summed(w, dist, 1, 0).astype(bf16)
            go(cross_copy(w, dist))

    def crossed(w, dist):
        cross_copy(w, dist).wait_recv()
        return summed(w, dist, 0, 0) + cross_in[w, dist, 0 : CROSSED[w]].astype(f32)

    def middle(w):
        return (CROSSED[w] // 2 + 15) // 16 * 16

    def merges(lane, direction):
        return lane < 2 and direction != lane

    def hop(w, lane, direction, dist):
        at = (w, lane, direction, dist)
        to = place.up if direction == 0 else place.down
        if dist == 1:
            src = near_out.at[w, direction, lane] if merges(lane, direction) else hop_in.at[w, direction, 0, lane]
            dst = last_in.at[w, direction, 0, lane]
        elif dist == 0:
            src, dst = near_out.at[w, direction, lane], last_in.at[w, direction, 1, lane]
        else:
            src, dst = hop_out.at[w, direction, dist - 2, lane], hop_in.at[w, direction, dist - 2, lane]
        if lane < 2:
            span = pl.ds(0, PADDED - CROSSED[w])
        elif dist == 4:
            span = pl.ds(0, middle(w)) if direction == 0 else pl.ds(middle(w), CROSSED[w] - middle(w))
        else:
            span = pl.ds(0, CROSSED[w])
        src, dst = src.at[span], dst.at[span]
        return src, dst, remote(src, dst, rsend.at[at], rrecv.at[at], to)

    def far(direction, dist):
        return dist if direction == 0 else NZ - dist

    def near_z(w):
        for piece in (1, 0):
            src, _, copy = hop(w, piece, piece, 0)
            src[...] = summed(w, far(piece, 1), piece, 1).astype(bf16)
            go(copy)

    def near_x(w):
        for direction in range(2):
            src, _, copy = hop(w, 2, direction, 0)
            src[...] = crossed(w, far(direction, 1)).astype(bf16)
            go(copy)

    def pass_on(w, lane):
        for direction in range(2):
            _, arrived, before = hop(w, lane, direction, 2)
            before.wait_recv()
            src, _, copy = hop(w, lane, direction, 1)
            if merges(lane, direction):
                src[...] = (summed(w, far(direction, 1), lane, 1) + arrived[...].astype(f32)).astype(bf16)
            go(copy)

    def ring_z(w, dist):
        for piece in (1, 0):
            for direction in range(2):
                if not exists(direction, dist, piece):
                    continue
                total = summed(w, far(direction, dist), piece, 1)
                if exists(direction, dist + 1, piece):
                    _, arrived, copy = hop(w, piece, direction, dist + 1)
                    copy.wait_recv()
                    total = total + arrived[...].astype(f32)
                src, _, copy = hop(w, piece, direction, dist)
                src[...] = total.astype(src.dtype)
                go(copy)

    def ring_x(w, dist):
        own_sum = crossed(w, 4) if dist == 4 else None
        for direction in range(2):
            src, _, copy = hop(w, 2, direction, dist)
            if dist == 4:
                src[...] = (own_sum[: middle(w)] if direction == 0 else own_sum[middle(w) :]).astype(src.dtype)
            else:
                _, arrived, before = hop(w, 2, direction, dist + 1)
                total = crossed(w, far(direction, dist))
                before.wait_recv()
                if dist == 3:
                    low, high = total[: middle(w)], total[middle(w) :]
                    if direction == 0:
                        low = low + arrived[...].astype(f32)
                    else:
                        high = high + arrived[...].astype(f32)
                    src[0 : middle(w)] = low.astype(src.dtype)
                    src[middle(w) : CROSSED[w]] = high.astype(src.dtype)
                else:
                    src[...] = (total + arrived[...].astype(f32)).astype(src.dtype)
            go(copy)

    def last_hops(w, lane, total):
        for direction in range(2):
            for dist in (1,) if merges(lane, direction) else (0, 1):
                _, arrived, copy = hop(w, lane, direction, dist)
                copy.wait_recv()
                total = total + arrived[...].astype(f32)
        return total

    def swap_copy(w):
        span = pl.ds(0, PADDED - CROSSED[w])
        return remote(x_out.at[w].at[span], x_in.at[w].at[span], ysend.at[w], yrecv.at[w], place.across)

    def turn(w):
        x_out[w, 0 : PADDED - CROSSED[w]] = last_hops(w, 1, summed(w, 0, 1, 1))
        go(swap_copy(w))

    def finish(w):
        total = last_hops(w, 2, crossed(w, 0))
        cut = CROSSED[w]
        update[w, 0:cut, 0, :] = rate_rows[w, 0:cut, :] * total
        total = last_hops(w, 0, summed(w, 0, 0, 1))
        swap_copy(w).wait_recv()
        total = total + x_in[w, 0 : PADDED - cut]
        update[w, cut:ROWS, 0, :] = rate_rows[w, cut:ROWS, :] * total[0 : ROWS - cut]

    def scatter(w):
        cross(w, 4, 3, 5)
        ring_z(w, 4)
        yield 1
        cross(w, 2, 6)
        near_z(w)
        yield 2
        ring_z(w, 3)
        yield 3
        ring_x(w, 4)
        cross(w, 1, 7, 0)
        yield 4
        ring_z(w, 2)
        ring_x(w, 3)
        yield 5
        near_x(w)
        pass_on(w, 1)
        pass_on(w, 0)
        ring_x(w, 2)
        yield 6
        turn(w)
        yield 7
        pass_on(w, 2)
        yield 8
        finish(w)
        yield 9

    def rows(index, size=UNIT):
        return pl.ds(index * size, size)

    def fold(values):
        return values.reshape(values.shape[0] // 8, 8, C).sum(axis=0)

    def spread(sums):
        column = sums.sum(axis=0, keepdims=True)
        top = column.astype(bf16)
        rest = column - top.astype(f32)
        middle = rest.astype(bf16)
        low = (rest - middle.astype(f32)).astype(bf16)
        terms = jnp.concatenate([top, middle, low, jnp.zeros((13, C), bf16)], axis=0)
        total = jnp.dot(terms, same_group[...], preferred_element_type=f32)
        return total.sum(axis=0, keepdims=True) * (1.0 / (POINTS * PER_GROUP))

    def sweep(body, start):
        return lax.fori_loop(0, FRAMES, lambda i, carry: body(pl.ds(pl.multiple_of(i * HW, HW), HW), carry), start)

    def padded(i):
        return pl.ds(HW + i * UNIT, UNIT)

    def silu(v):
        return v / (1.0 + jnp.exp(-v))

    loads[0].wait()
    centre = spread(sweep(lambda at, acc: acc + fold(clip[at, :].astype(f32)), zero))

    def squares(ref, mean):
        def body(at, acc):
            off = ref[at, :].astype(f32) - mean
            return acc + fold(off * off)

        return lax.rsqrt(spread(sweep(body, zero)) + 1e-05)

    inverse = squares(clip, centre)
    units = POINTS // UNIT

    def act_unit(i):
        values = (clip[rows(i), :].astype(f32) - centre) * inverse
        act_one[padded(i), :] = silu(values).astype(bf16)

    def flip_unit(flipped, ref, i):
        flipped[:, rows(i)] = ref[padded(i), :].T

    ring_start(0)
    group_send(1)
    loads[2].start()
    for i in range(4):
        act_unit(i)
    ring_step(0, 1)
    ring_start(1)
    act_unit(4)
    act_unit(5)
    ring_step(0, 2)
    ring_step(1, 1)
    act_unit(6)
    ring_sides(0, 1)
    loads[1].wait()
    half_width = freqs.shape[1]
    angles = t_ref[0].astype(f32) * freqs[...]
    person = table[pl.ds(ident_ref[0], 1), :]
    embedding = jnp.concatenate([jnp.cos(angles), jnp.sin(angles)], axis=1) + person
    embed = jnp.broadcast_to(silu(embedding).astype(bf16), (16, 2 * half_width))
    bias = jnp.dot(embed, proj[...], preferred_element_type=f32)[0:1]
    ring_step(0, 3)
    ring_step(1, 2)
    for i in range(3):
        flip_unit(flip_one, act_one, i)
    ring_sides(0, 2)
    ring_step(0, 4)
    ring_step(1, 3)
    ring_sides(1, 1)
    for i in range(3, units):
        flip_unit(flip_one, act_one, i)
    ring_sides(0, 3)
    ring_sides(0, 4)
    ring_step(1, 4)
    ring_sides(1, 2)
    dense(0)

    def stacked(ref, start, size, taps):
        return jnp.concatenate([ref[pl.ds(start + HW * tap, size), :] for tap in taps], axis=1)

    half = POINTS // 2
    sums = zero
    for part in range(2):
        mixed = jnp.dot(stacked(act_one, part * half, half, (0, 1, 2)), weights[0], preferred_element_type=f32)
        values = SCALE * mixed + bias
        hid[pl.ds(part * half, half), :] = values
        sums = sums + fold(values)
        ring_sides(1, 3 + part)
    for step in range(1, N_GROUP):
        go(rate_copy(step, True))
    centre_two = spread(sums)
    inverse_two = squares(hid, centre_two)
    for i in range(units):
        values = (hid[rows(i), :] - centre_two) * inverse_two
        hid[rows(i), :] = values
        act_two[padded(i), :] = silu(values).astype(bf16)
    for i in range(units):
        flip_unit(flip_two, act_two, i)
    dense(1)
    loads[2].wait()

    for part in range(2):
        at = pl.ds(part * half, half)
        mixed = jnp.dot(stacked(act_two, part * half, half, (0, 1, 2)), weights[1], preferred_element_type=f32)
        output = clip[at, :].astype(f32) + SCALE * mixed
        err[pl.ds(HW + part * half, half), :] = (output - target[at, :].astype(f32)).astype(bf16)

    def weight_grad(flipped, ref, tap):
        grad[C * tap : C * (tap + 1), :] = jnp.dot(
            flipped[...], ref[pl.ds(HW * (2 - tap), POINTS), :], preferred_element_type=f32
        )

    ready = (0, 5, 10, 16)
    for tap in range(3):
        weight_grad(flip_two, err, tap)
        pair(1, ready[tap], ready[tap + 1])

    scatter_two = scatter(1)
    sum_grad, sum_mixed = zero, zero
    for part in range(2):
        at = pl.ds(part * half, half)
        back = jnp.zeros((half, C), f32)
        for tap in range(3):
            back = back + lax.dot_general(
                err[pl.ds(part * half + HW * (2 - tap), half), :],
                weights[1, C * tap : C * (tap + 1), :],
                (((1,), (1,)), ((), ())),
                preferred_element_type=f32,
            )
        values = hid[at, :]
        gate = 1.0 / (1.0 + jnp.exp(-values))
        inner = (SCALE * back) * (gate * (1.0 + values * (1.0 - gate)))
        grad[at, :] = inner
        sum_grad = sum_grad + fold(inner)
        sum_mixed = sum_mixed + fold(inner * values)
        next(scatter_two)
        if part:
            next(scatter_two)
    mean_grad, mean_mixed = spread(sum_grad), spread(sum_mixed)
    for i in range(units):
        inner = grad[rows(i), :] - mean_grad - hid[rows(i), :] * mean_mixed
        grad_hid[padded(i), :] = (inner * inverse_two).astype(bf16)
    next(scatter_two)
    for tap in range(3):
        weight_grad(flip_one, grad_hid, tap)
        pair(0, ready[tap], ready[tap + 1])
        if tap == 1:
            next(scatter_two)
    scatter_one = scatter(0)
    early = 28
    next(scatter_one)
    next(scatter_one)
    settle(early)
    next(scatter_two)
    settle(early)
    next(scatter_one)
    settle(early)
    next(scatter_one)
    for step in range(1, N_GROUP):
        rate_copy(step, False).wait_recv()
    for w in range(2):
        rate_rows[w] = assemble(lambda group: rbuf[w, group]) * SCALE
    next(scatter_one)
    settle(early)
    next(scatter_two)
    next(scatter_two)
    settle(early)
    next(scatter_one)
    next(scatter_two)
    settle(early)
    next(scatter_one)
    settle(early)
    next(scatter_one)
    settle(early // 2)
    next(scatter_one)
    settle(len(sends))


def step(timestep, identity, freqs, table, clip, target, time_proj, w1, w2, r1, r2):
    f32, bf16 = jnp.float32, jnp.bfloat16
    dma = pltpu.SemaphoreType.DMA
    vmem = pl.BlockSpec(memory_space=pltpu.VMEM)
    smem = pl.BlockSpec(memory_space=pltpu.SMEM)
    anywhere = pl.BlockSpec(memory_space=pl.ANY)
    part = (max(CROSSED), C)
    wide = (POINTS + 2 * HW, C)
    rows = jax.ShapeDtypeStruct((2, ROWS, 1, C), f32)
    return pl.pallas_call(
        step_kernel,
        out_shape=(rows, rows),
        in_specs=[smem] * 2 + [vmem] * 2 + [anywhere] * 3 + [vmem] * 4,
        out_specs=(vmem,) * 2,
        scratch_shapes=[
            pltpu.VMEM((POINTS, C), bf16),
            pltpu.VMEM((POINTS, C), bf16),
            pltpu.VMEM(time_proj.shape, bf16),
            pltpu.VMEM((C, C), bf16),
            pltpu.VMEM(wide, bf16),
            pltpu.VMEM(wide, bf16),
            pltpu.VMEM(wide, bf16),
            pltpu.VMEM(wide, bf16),
            pltpu.VMEM((C, POINTS), bf16),
            pltpu.VMEM((C, POINTS), bf16),
            pltpu.VMEM((POINTS, C), f32),
            pltpu.VMEM((2, TAPS, C), bf16),
            pltpu.VMEM((TAPS + 8, C), f32),
            pltpu.VMEM((2, NX, N_GROUP, ROWS, COLS), bf16),
            pltpu.VMEM((2, N_GROUP, ROWS, COLS), bf16),
            pltpu.VMEM((2, NZ, NC, NX, 4, 16, C), bf16),
            pltpu.VMEM((2, NX, NZ, NC, PADDED, C), f32),
            pltpu.VMEM((2, NX, NZ, PADDED, C), f32),
            pltpu.VMEM((2, NZ) + part, bf16),
            pltpu.VMEM((2, NZ) + part, bf16),
            pltpu.VMEM((2, 2, 3, 3) + part, bf16),
            pltpu.VMEM((2, 2, 3, 3) + part, bf16),
            pltpu.VMEM((2, 2, 3) + part, bf16),
            pltpu.VMEM((2, 2, 2, 3) + part, bf16),
            pltpu.VMEM((2,) + part, f32),
            pltpu.VMEM((2,) + part, f32),
            pltpu.VMEM((2, ROWS, C), f32),
            dma((3,)),
            dma((2, 2, N_GROUP)),
            dma((2, 2, N_GROUP)),
            dma((N_GROUP,)),
            dma((N_GROUP,)),
            dma((2, 2, 5, 2)),
            dma((2, 2, 5, 2)),
            dma((2, 2, NZ)),
            dma((2, 2, NZ)),
            dma((2, 2, NZ)),
            dma((2, 2, NZ)),
            dma((2, 2)),
            dma((2, 2)),
            dma((2, 3, 2, 5)),
            dma((2, 3, 2, 5)),
            dma((2,)),
            dma((2,)),
            dma((2, NX, NZ)),
            dma((2, NX, NZ)),
            dma((2, NZ)),
            dma((2, NZ)),
        ],
        compiler_params=pltpu.CompilerParams(
            collective_id=0, has_side_effects=True, vmem_limit_bytes=62 << 20
        ),
        name="inner_step",
    )(timestep, identity, freqs, table, clip, target, time_proj, w1, w2, r1, r2)


def shards(
    clips,
    targets,
    timestep,
    identity,
    conv1_weight,
    conv2_weight,
    rate1,
    rate2,
    time_proj,
    subject_table,
):
    half_width = subject_table.shape[1] // 2
    freqs = np.exp(-math.log(10000.0) * np.arange(half_width) / half_width).astype(np.float32)
    update, kept = step(
        timestep,
        identity,
        freqs[None],
        subject_table,
        clips.reshape(POINTS, C),
        targets.reshape(POINTS, C),
        time_proj,
        conv1_weight,
        conv2_weight,
        rate1,
        rate2,
    )
    return tuple((kept[w] - update[w]).transpose(1, 0, 2) for w in range(2))


def solution(mesh):
    return jax.shard_map(
        shards,
        mesh=mesh,
        in_specs=(
            P(("group", "member"), None, None, None),
            P(("group", "member"), None, None, None),
            P(("group", "member")),
            P(("group", "member")),
            P("member", "group"),
            P("member", "group"),
            P("member", "group"),
            P("member", "group"),
            P(),
            P(),
        ),
        out_specs=(P("group", "member", None), P("group", "member", None)),
        check_vma=False,
    )
```
